256 devices in a mesh: row: 8 (over z_hi, x), col: 32 (over y, z_lo, core).
Axes of the slice: x: 4, y: 4, z: 8 (z_hi: 2, z_lo: 4; z = z_hi * 4 + z_lo), core: 2. Of those that a mesh axis runs over, the one named last changes fastest.
Arguments:
- inv_anc: float32 [8, 32, 48, 12288], P(None, 'col', None, 'row'), may hold values from -6 to 6, as said below
- factor_cols: float32 [4, 12288, 256], P(None, ('row', 'col')), may hold values from -0.0546875 to 0.0546875
- couple: float32 [6, 256, 256], replicated, may hold values from -0.1875 to 0.1875
- diag_inv: float32 [4, 256, 256], replicated, may hold values from -6 to 6, as said below
- pattern: int32 [4, 48], replicated, may hold values 0 or 1
- parent: int32 [4], replicated, may hold values from 0 to 4, as said below
Outputs:
- inv_cols: float32 [4, 12288, 256], P(None, ('row', 'col'))
- win_cols: float32 [6, 256, 256], replicated
- win_diag: float32 [4, 256, 256], replicated
The draws below stay inside these ranges and needn't reach their ends.
Inputs may be any that keep to these rules, and one draw needn't show every extreme that they name: parent[0] is 4, meaning a parent in the ancestor set; for j of 1 or more parent[j] is an earlier supernode or 4. The matrix full built from inv_anc as in the reference program is symmetric. Each diag_inv[j] is symmetric.
All inputs are finite; a program needn't handle non-finite values.
Results may differ from the reference program's by a relative error of at most 0.0001.
Values sent between devices are 32-bit elements; how exact they have to be, the bound alone decides.
No kernel may reach another device: no remote copies, remote signals or barrier semaphores. Data moves between devices by JAX's collectives and lax.ppermute only.
A program may use at most 64 MiB of HBM per device.

```python
import jax
import jax.numpy as jnp
from jax import lax

W = 256
NSUP = 4
RW = 48
NS = 12288
NB = 48
NPAIR = 6
N_ROW = 8
N_COL = 32


def draw_parent(key, part):
    random_values = jax.random.randint(jax.random.fold_in(key, 37), (NSUP,), 0, 1 << 20)
    positions = jnp.arange(NSUP, dtype=jnp.int32)
    picked = random_values % (positions + 1)
    parent = jnp.where(picked == positions, NSUP, picked)
    parent = parent.at[0].set(NSUP)
    second_free = parent[1] == NSUP
    parent = parent.at[2].set(jnp.where(second_free, 0, parent[2]))
    return parent.astype(jnp.int32)


def symmetric_draw(key, shape):
    raw = jax.random.normal(key, shape, jnp.float32)
    raw = jnp.clip(raw, -4.0, 4.0)
    return (raw + jnp.swapaxes(raw, -1, -2)) * 0.70710678


def draw_inv_anc(key, part):
    full = symmetric_draw(jax.random.fold_in(key, 11), (NS, NS))
    return full.reshape(N_ROW, N_COL, RW, NS).astype(jnp.float32)


def draw_diag_inv(key, part):
    return symmetric_draw(jax.random.fold_in(key, 23), (NSUP, W, W)).astype(jnp.float32)


def touch_ends(result, stream_key, least, top_value):
    index_at = [jax.random.randint(jax.random.fold_in(stream_key, axis), (), 0, length) for axis, length in enumerate(result.shape)]
    widest = result.shape.index(max(result.shape))
    neighbour = index_at[:widest] + [(index_at[widest] + 1) % result.shape[widest]] + index_at[widest + 1:]
    return result.at[tuple(index_at)].set(least).at[tuple(neighbour)].set(top_value)


def levels(stream_key, shape, shards, smallest, largest):
    level, own = 1.0, jax.random.fold_in(stream_key, 6)
    for dim, blocks in shards:
        draws = jnp.exp(jax.random.uniform(jax.random.fold_in(own, dim), (blocks,), jnp.float32, smallest / len(shards), largest / len(shards)))
        level = level * jnp.repeat(draws, shape[dim] // blocks).reshape([-1 if axis == dim else 1 for axis in range(len(shape))])
    return level


def gaussian(own_key, shape, scale, limit, pieces=(), held_as=jnp.bfloat16):
    gain = levels(own_key, shape, pieces, -0.22, 0.18) if pieces else 1.0
    values = jax.random.normal(own_key, shape, jnp.float32) * scale * gain
    return jnp.minimum(jnp.maximum(values, -limit), limit).astype(held_as)


def setup_inputs(seed: int = 0) -> dict:
    splits = jax.random.split(jax.random.key(seed), 7)
    return {
        "inv_anc": draw_inv_anc(jax.random.fold_in(splits[6], 71), 0),
        "factor_cols": gaussian(splits[1], (NSUP, NS, W), NS ** -0.5, 0.0546875, ((1, 256),), jnp.float32),
        "couple": gaussian(splits[2], (NPAIR, W, W), (4 * W) ** -0.5, 0.1875, (), jnp.float32),
        "diag_inv": draw_diag_inv(jax.random.fold_in(splits[6], 71), 0),
        "pattern": touch_ends((jax.random.randint(splits[4], (NSUP, NB), 0, 4) < 3).astype(jnp.int32), jax.random.fold_in(splits[4], 1), 0, 1),
        "parent": draw_parent(jax.random.fold_in(splits[6], 71), 0),
    }


exact_mode = lax.Precision.HIGHEST


def product(left, right):
    return jnp.dot(left, right, precision=exact_mode, preferred_element_type=jnp.float32)


def ancestry(parent):
    linked = {}
    for j in range(NSUP):
        for m in range(j):
            linked_now = parent[j] == m
            for p in range(m + 1, j):
                linked_now = linked_now | ((parent[j] == p) & linked[(p, m)])
            linked[(j, m)] = linked_now
    return linked


def couplings(couple, parent):
    linked = ancestry(parent)
    blocks = {}
    for j in range(NSUP):
        for m in range(j):
            blocks[(j, m)] = couple[j * (j - 1) // 2 + m] * linked[(j, m)].astype(jnp.float32)
    return blocks


def window_blocks(crossed, diag_terms, diag_inv, blocks):
    off_diag = {}
    diagonal = []

    def lookup_block(first, second):
        if first == second:
            return diagonal[first]
        if first < second:
            return off_diag[(second, first)]
        return off_diag[(first, second)].T

    for j in range(NSUP):
        for m in range(j):
            running = crossed[(j, m)]
            for q in range(j):
                running = running + product(lookup_block(m, q), blocks[(j, q)])
            off_diag[(j, m)] = -running
        diag_value = diag_inv[j] - diag_terms[j]
        for m in range(j):
            diag_value = diag_value - product(blocks[(j, m)].T, off_diag[(j, m)])
        diagonal.append(diag_value)
    pair_list = [off_diag[(j, m)] for j in range(NSUP) for m in range(j)]
    return jnp.stack(pair_list), jnp.stack(diagonal)


def reference(inv_anc, factor_cols, couple, diag_inv, pattern, parent):
    full_matrix = inv_anc.reshape(NS, NS)
    row_mask = jnp.repeat(pattern.astype(jnp.float32), W, axis=1)
    masked = factor_cols * row_mask[:, :, None]
    blocks = couplings(couple, parent)
    columns = []
    for j in range(NSUP):
        running = product(full_matrix, masked[j])
        for m in range(j):
            running = running + product(columns[m], blocks[(j, m)])
        columns.append(-running)
    crossed = {}
    diag_terms = []
    for j in range(NSUP):
        for m in range(j):
            crossed[(j, m)] = product(columns[m].T, masked[j])
        diag_terms.append(product(masked[j].T, columns[j]))
    pair_blocks, diagonal = window_blocks(crossed, diag_terms, diag_inv, blocks)
    return jnp.stack(columns), pair_blocks, diagonal
```

```python
import jax
import jax.numpy as jnp
from jax import lax
from jax.sharding import PartitionSpec as P

W = 256
NSUP = 4
SIZES = {"zh": 2, "x": 4, "y": 4, "zl": 4, "c": 2}
BOTH = ("row", "col")
HIGH = lax.Precision.HIGH
FULL = lax.Precision.HIGHEST


def product(left, right, precision=FULL):
    return jnp.dot(left, right, precision=precision, preferred_element_type=jnp.float32)


def product_t(left, right, precision=FULL):
    return lax.dot_general(
        left, right, (((0,), (0,)), ((), ())), precision=precision, preferred_element_type=jnp.float32
    )


def place():
    row, col = lax.axis_index("row"), lax.axis_index("col")
    return {"zh": row >> 2, "x": row & 3, "y": col >> 3, "zl": col >> 1 & 3, "c": col & 1}


def moved(value, axis, step):
    names = list(SIZES)
    perm = []
    for device in range(256):
        rest, at = device, {}
        for name in reversed(names):
            at[name] = rest % SIZES[name]
            rest //= SIZES[name]
        at[axis] = (at[axis] + step) % SIZES[axis]
        target = 0
        for name in names:
            target = target * SIZES[name] + at[name]
        perm.append((device, target))
    return lax.ppermute(value, BOTH, perm)


def scatter_sum(value, at, axis):
    n = SIZES[axis]
    rows = value.shape[0] // n
    mine = at[axis]
    part = lambda k: lax.dynamic_slice_in_dim(value, ((mine + k) & (n - 1)) * rows, rows, 0)
    got = [moved(part(k), axis, k) for k in range(1, n)]
    total = part(0)
    for piece in got:
        total = total + piece
    return total


def gather(value, at, axis):
    n = SIZES[axis]
    rows = value.shape[0]
    got = [value] + [moved(value, axis, k) for k in range(1, n)]
    whole = jnp.zeros((n * rows,) + value.shape[1:], value.dtype)
    for k, piece in enumerate(got):
        whole = lax.dynamic_update_slice_in_dim(whole, piece, ((at[axis] - k) & (n - 1)) * rows, 0)
    return whole


def couplings(couple, parent):
    linked = {}
    blocks = {}
    for j in range(NSUP):
        for m in range(j):
            now = parent[j] == m
            for p in range(m + 1, j):
                now = now | (parent[j] == p) & linked[p, m]
            linked[j, m] = now
            blocks[j, m] = couple[j * (j - 1) // 2 + m] * now.astype(jnp.float32)
    return blocks


def shards(inv_anc, factor_cols, couple, diag_inv, pattern, parent):
    at = place()
    rows = factor_cols.shape[1]
    local = inv_anc.reshape(-1, inv_anc.shape[3])
    first = (lax.axis_index("row") * 32 + lax.axis_index("col")) * rows
    ids = (first + jnp.arange(rows, dtype=jnp.int32)) >> 8
    picked = ids[None, :, None] == jnp.arange(pattern.shape[1], dtype=jnp.int32)[None, None, :]
    mask = jnp.sum(jnp.where(picked, pattern[:, None, :], 0), axis=2).astype(jnp.float32)
    masked = factor_cols * mask[:, :, None]
    blocks = couplings(couple, parent)

    solved = []
    for j in range(NSUP):
        value = masked[j]
        for m in range(j):
            value = value - product(solved[m], blocks[j, m])
        solved.append(value)
    own = jnp.concatenate(solved, axis=1)

    near = gather(own, at, "zl")
    left, right = moved(near, "y", 1), moved(near, "y", 3)
    half = near.shape[0] // 2
    far_a, far_b = moved(left[:half], "y", 1), moved(right[half:], "y", 3)
    mine = [near, left, right, far_a, far_b]
    other = [moved(v, "c", 1) for v in mine]
    stacked = jnp.concatenate(mine + other, axis=0)

    split = local.reshape(-1, 4, 4, 2, rows).transpose(3, 1, 0, 2, 4).reshape(2, 4, -1, 4 * rows)
    ordered = []
    for par in range(2):
        here = lax.dynamic_index_in_dim(split, at["c"] ^ par, 0, keepdims=False)
        for k in (0, 1, 3, 2):
            ordered.append(lax.dynamic_index_in_dim(here, (at["y"] - k) & 3, 0, keepdims=False))
    ordered = jnp.concatenate(ordered, axis=1)

    pair = jnp.stack([own, moved(own, "zh", 1)])
    pair = jnp.where(at["zh"] == 0, pair, pair[::-1])
    quads = [pair] + [moved(pair, "x", k) for k in range(1, 4)]
    spread = jnp.zeros((2, 4) + own.shape, own.dtype)
    for k, piece in enumerate(quads):
        spread = lax.dynamic_update_slice_in_dim(spread, piece[:, None], (at["x"] - k) & 3, 1)
    beside = spread.reshape(8 * rows, -1)

    partial_value = product(ordered, stacked, HIGH)

    pieces = [product_t(beside[:, : (j + 1) * W], partial_value[:, j * W : (j + 1) * W], HIGH) for j in range(NSUP)]
    window = jnp.concatenate(pieces, axis=0)
    lanes = W // 2
    kept = lax.dynamic_slice_in_dim(window, at["c"] * lanes, lanes, 1)
    given = lax.dynamic_slice_in_dim(window, (1 - at["c"]) * lanes, lanes, 1)
    total = kept + moved(given, "c", 1)
    total = scatter_sum(total, at, "y")
    total = scatter_sum(total, at, "x")
    total = scatter_sum(total, at, "zl")
    total = total + moved(total, "zh", 1)
    total = gather(total, at, "zl")
    total = gather(total, at, "x")
    total = gather(total, at, "y")
    twin = moved(total, "c", 1)
    low = jnp.where(at["c"] == 0, total, twin)
    top = jnp.where(at["c"] == 0, twin, total)
    window = jnp.concatenate([low, top], axis=1)

    inverse = {}
    for j in range(NSUP):
        for m in range(j):
            value = -blocks[j, m]
            for q in range(m + 1, j):
                value = value - product(inverse[m, q], blocks[j, q])
            inverse[m, j] = value
    scaled = {}
    for q in range(NSUP):
        scaled[q, q] = diag_inv[q]
        for j in range(q + 1, NSUP):
            scaled[q, j] = product(diag_inv[q], inverse[q, j])
    base = []
    for j in range(NSUP):
        for m in range(j + 1):
            value = scaled[m, j]
            for q in range(m):
                value = value + product_t(inverse[q, m], scaled[q, j])
            base.append(value)
    window = window.reshape(-1, W, W) + jnp.stack(base)
    order = [(j, m) for j in range(NSUP) for m in range(j + 1)]
    pair_blocks = jnp.stack([window[order.index((j, m))] for j in range(NSUP) for m in range(j)])
    diagonal = jnp.stack([window[order.index((j, j))] for j in range(NSUP)])

    grid = partial_value.reshape(2, 4, rows, -1)
    part = lambda k: lax.dynamic_index_in_dim(grid, (at["x"] + k) & 3, 1, keepdims=False)
    summed = part(0)
    for piece in [moved(part(k), "x", k) for k in range(1, 4)]:
        summed = summed + piece
    keep = lax.dynamic_index_in_dim(summed, at["zh"], 0, keepdims=False)
    give = lax.dynamic_index_in_dim(summed, 1 - at["zh"], 0, keepdims=False)
    columns = -(keep + moved(give, "zh", 1))
    columns = jnp.stack([columns[:, j * W : (j + 1) * W] for j in range(NSUP)])
    return (columns, pair_blocks, diagonal)


def solution(mesh):
    in_specs = (P(None, "col", None, "row"), P(None, BOTH, None), P(), P(), P(), P())
    out_specs = (P(None, BOTH, None), P(), P())
    return jax.shard_map(shards, mesh=mesh, in_specs=in_specs, out_specs=out_specs, check_vma=False)
```

```python
import functools

import jax
import jax.numpy as jnp
from jax import lax
from jax.experimental import pallas as pl
from jax.experimental.pallas import tpu as pltpu
from jax.sharding import PartitionSpec as P

W = 256
NSUP = 4
RW = 48
HALF = W // 2
SIZES = {"zh": 2, "x": 4, "y": 4, "zl": 4, "c": 2}
BOTH = ("row", "col")
CHUNKS = ((0, 1, 2, 3),)
F32, BF16 = jnp.float32, jnp.bfloat16
PAIRS = [(m, j) for j in range(NSUP) for m in range(j)]
ALL_BLOCKS = PAIRS + [(j, j) for j in range(NSUP)]
VMEM = pl.BlockSpec(memory_space=pltpu.VMEM)
SMEM = pl.BlockSpec(memory_space=pltpu.SMEM)


def place():
    row, col = lax.axis_index("row"), lax.axis_index("col")
    return {"zh": row >> 2, "x": row & 3, "y": col >> 3, "zl": (col >> 1) & 3, "c": col & 1}


def moved(value, axis, step):
    return sent(value, axis, lambda a: (a + step) % SIZES[axis])


def sent(value, axis, rule):
    names = list(SIZES)
    perm = []
    for device in range(256):
        rest, at = device, {}
        for name in reversed(names):
            at[name] = rest % SIZES[name]
            rest //= SIZES[name]
        at[axis] = rule(at[axis])
        target = 0
        for name in names:
            target = target * SIZES[name] + at[name]
        perm.append((device, target))
    return lax.ppermute(value, BOTH, perm)


def tie(*values):
    return lax.optimization_barrier(values)


def halves(value):
    top = value.astype(BF16)
    return top, (value - top.astype(F32)).astype(BF16)


def mul(left, right, over=(1, 0)):
    dims = (((over[0],), (over[1],)), ((), ()))
    dot = lambda u, v: lax.dot_general(u, v, dims, preferred_element_type=F32)
    return dot(left[0], right[0]) + (dot(left[1], right[0]) + dot(left[0], right[1]))


def couplings(couple, parent):
    linked = {}
    blocks = {}
    for j in range(NSUP):
        for m in range(j):
            now = parent[j] == m
            for p in range(m + 1, j):
                now = now | ((parent[j] == p) & linked[p, m])
            linked[j, m] = now
            blocks[j, m] = couple[j * (j - 1) // 2 + m] * jnp.where(now, 1.0, 0.0).astype(F32)
    return blocks


def pre_kernel(parent, pattern, factor, couple, out):
    first = (lax.axis_index("row") * 32 + lax.axis_index("col")) * RW
    block = first >> 8
    after = jnp.minimum(block + 1, pattern.shape[1] - 1)
    edge = (block + 1) * W - first
    low = lax.broadcasted_iota(jnp.int32, (RW, W), 0) < edge
    blocks = couplings(couple, parent)
    values = []
    for j in range(NSUP):
        here, there = pattern[j, block].astype(F32), pattern[j, after].astype(F32)
        values.append(factor[j] * jnp.where(low, here, there))
    for m in range(NSUP):
        out[:, m * W : (m + 1) * W] = values[m]
        left = halves(values[m])
        for j in range(m + 1, NSUP):
            values[j] = values[j] - mul(left, halves(blocks[j, m]))


def base_kernel(order, parent, couple, diag_inv, out, *held):
    chigh, clow, ihigh, ilow, shigh, slow = held
    at = lambda q, j: order.index((q, j))

    def keep(high, low, i, value):
        high[i], low[i] = halves(value)

    def kept(high, low, i):
        return high[i], low[i]

    for (j, m), value in couplings(couple, parent).items():
        keep(chigh, clow, at(m, j), value)
        keep(ihigh, ilow, at(m, j), -value)
    for gap in range(2, NSUP):
        for m in range(NSUP - gap):
            j = m + gap
            value = -(chigh[at(m, j)].astype(F32) + clow[at(m, j)].astype(F32))
            for q in range(m + 1, j):
                value = value - mul(kept(ihigh, ilow, at(m, q)), kept(chigh, clow, at(q, j)))
            keep(ihigh, ilow, at(m, j), value)
    for q in range(NSUP):
        out[at(q, q) * W : (at(q, q) + 1) * W, :] = diag_inv[q]
        keep(shigh, slow, at(q, q), diag_inv[q])
        for j in range(q + 1, NSUP):
            i = at(q, j)
            value = mul(kept(shigh, slow, at(q, q)), kept(ihigh, ilow, i))
            out[i * W : (i + 1) * W, :] = value
            keep(shigh, slow, i, value)
    for i, (m, j) in enumerate(order):
        rows = slice(i * W, (i + 1) * W)
        for q in range(m):
            out[rows, :] = out[rows, :] + mul(kept(ihigh, ilow, at(q, m)), kept(shigh, slow, at(q, j)), (0, 0))


def main_kernel(chunk, order, skip, *refs):
    local, base = refs[0], refs[1]
    mine, other, quads = refs[2:7], refs[7:12], refs[12:16]
    outs = refs[16:20]
    kept, given = refs[20], refs[21]
    top, bot, rtop, rbot, result = refs[22:27]
    at = place()
    for par, pieces in enumerate((mine, other)):
        core = at["c"] ^ par
        for piece, k, start in zip(pieces, (0, 1, 3, 2, 2), (0, 0, 0, 0, 2)):
            ya = (at["y"] - k) & 3
            for r in range(piece.shape[0] // RW):
                za = (at["zl"] - r - start) & 3
                dst = pl.multiple_of(((ya * 4 + za) * 2 + core) * RW, 16)
                hi, lo = halves(piece[r * RW : (r + 1) * RW, :])
                top[pl.ds(dst, RW), :] = hi
                bot[pl.ds(dst, RW), :] = lo
    for k, piece in enumerate(quads):
        xa = (at["x"] - k) & 3
        for r in range(2):
            dst = pl.multiple_of(((at["zh"] ^ r) * 4 + xa) * RW, 16)
            hi, lo = halves(piece[r])
            rtop[pl.ds(dst, RW), :] = hi
            rbot[pl.ds(dst, RW), :] = lo
    value = mul(halves(local[...]), (top[...], bot[...]))
    result[...] = value
    for k, out in enumerate(outs):
        xa = (at["x"] + k) & 3
        for r in range(2):
            out[r] = result[pl.ds(pl.multiple_of((r * 4 + xa) * RW, 16), RW), :]
    lead = (lax.axis_index("row") == 0) & (lax.axis_index("col") == 0)
    split = halves(value)
    cols = lambda pair, s: tuple(v[:, s * W : (s + 1) * W] for v in pair)
    beside = lambda s: (rtop[:, s * W : (s + 1) * W], rbot[:, s * W : (s + 1) * W])
    for i, (m, j) in enumerate(order):
        if j in chunk:
            block = mul(beside(m), cols(split, chunk.index(j)), (0, 0))
        else:
            block = mul(cols(split, chunk.index(m)), beside(j), (0, 0))
        rows = slice(i * W, (i + 1) * W)
        block = block + jnp.where(lead, base[(skip + i) * W : (skip + i + 1) * W, :], 0.0)
        first, second = block[:, :HALF], block[:, HALF:]
        even = at["c"] == 0
        kept[rows, :] = jnp.where(even, first, second)
        given[rows, :] = jnp.where(even, second, first)


def join_kernel(axis, *refs):
    pieces, out = refs[:-1], refs[-1]
    at = place()[axis]
    rows = pieces[0].shape[0]
    for k, piece in enumerate(pieces):
        dst = pl.multiple_of(((at - k) & (SIZES[axis] - 1)) * rows, 8)
        out[pl.ds(dst, rows), :] = piece[...]


def add_split_kernel(axis, count, *refs):
    values, outs = refs[:count], refs[count:-1]
    whole = refs[-1]
    at = place()[axis]
    total = values[0][...]
    for value in values[1:]:
        total = total + value[...]
    whole[...] = total
    rows = outs[0].shape[0]
    for k, out in enumerate(outs):
        src = pl.multiple_of(((at + k) & (SIZES[axis] - 1)) * rows, 8)
        out[...] = whole[pl.ds(src, rows), :]


def final_kernel(orders, *refs):
    count = 8 * len(orders)
    pieces, pair_out, diag_out, wholes = refs[:count], refs[count], refs[count + 1], refs[count + 2 :]
    at = place()
    for i, order in enumerate(orders):
        whole = wholes[i]
        for par in range(2):
            for k in range(4):
                piece = pieces[i * 8 + par * 4 + k]
                rows = piece.shape[0]
                dst = pl.multiple_of(((at["y"] - k) & 3) * rows, 8)
                lane = pl.multiple_of((at["c"] ^ par) * HALF, HALF)
                whole[pl.ds(dst, rows), pl.ds(lane, HALF)] = piece[...]
        for b, (m, j) in enumerate(order):
            rows = slice(b * W, (b + 1) * W)
            if m == j:
                diag_out[j] = whole[rows, :]
            else:
                pair_out[PAIRS.index((m, j))] = whole[rows, :]


def kernel(body, args, out_shapes, scratch=(), smem=0, flops=0):
    single = not isinstance(out_shapes, list)
    return pl.pallas_call(
        body,
        out_shape=jax.ShapeDtypeStruct(out_shapes, F32)
        if single
        else [jax.ShapeDtypeStruct(s, F32) for s in out_shapes],
        in_specs=[SMEM] * smem + [VMEM] * (len(args) - smem),
        out_specs=VMEM if single else [VMEM] * len(out_shapes),
        scratch_shapes=[pltpu.VMEM(s, t) for s, t in scratch],
        compiler_params=pltpu.CompilerParams(vmem_limit_bytes=56 << 20),
        cost_estimate=pl.CostEstimate(
            flops=flops, transcendentals=0, bytes_accessed=sum(4 * a.size for a in args)
        ),
    )(*args)


def split_sum(values, axis):
    rows, width = values[0].shape
    n = SIZES[axis]
    return kernel(
        functools.partial(add_split_kernel, axis, len(values)),
        list(values),
        [(rows // n, width)] * n,
        [((rows, width), F32)],
    )


def scattered(pieces, axis):
    return [pieces[0]] + [moved(pieces[k], axis, k) for k in range(1, len(pieces))]


def gathered(value, axis):
    return [value] + [moved(value, axis, k) for k in range(1, SIZES[axis])]


def total_of(values):
    total = values[0]
    for value in values[1:]:
        total = total + value
    return total


def shards(inv_anc, factor_cols, couple, diag_inv, pattern, parent):
    at = place()
    local = inv_anc.reshape(-1, inv_anc.shape[3])
    height = local.shape[0]

    orders = []
    done = set()
    for chunk in CHUNKS:
        order = [b for b in ALL_BLOCKS if (b[0] in chunk or b[1] in chunk) and b not in done]
        done |= set(order)
        orders.append(order)

    own = kernel(
        pre_kernel, [parent, pattern, factor_cols, couple], (RW, NSUP * W), smem=2, flops=1 << 20
    )

    nears = []
    for chunk in CHUNKS:
        part = own[:, chunk[0] * W : (chunk[-1] + 1) * W]
        nears.append(jnp.concatenate(gathered(part, "zl"), axis=0))
    nears[0], later = tie(nears[0], own)

    pair = jnp.stack([later, moved(later, "zh", 1)])

    held = []
    for near in nears:
        left, right = moved(near, "y", 1), moved(near, "y", 3)
        half = near.shape[0] // 2
        far_a, far_b = moved(left[:half], "y", 1), moved(right[half:], "y", 3)
        mine = [near, left, right, far_a, far_b]
        held.append(mine + [moved(v, "c", 1) for v in mine])
    quads = gathered(pair, "x")

    couple_later, _ = tie(couple, nears[0])
    base = kernel(
        functools.partial(base_kernel, sum(orders, [])),
        [parent, couple_later, diag_inv],
        (len(ALL_BLOCKS) * W, W),
        [((len(ALL_BLOCKS), W, W), BF16)] * 6,
        smem=1,
        flops=1 << 31,
    )

    columns = []
    finals = []
    skip = 0
    for chunk, order, pieces in zip(CHUNKS, orders, held):
        width = len(chunk) * W
        tall = len(order) * W
        *parts, kept, given = kernel(
            functools.partial(main_kernel, chunk, order, skip),
            [local, base] + pieces + quads,
            [(2, RW, width)] * 4 + [(tall, HALF)] * 2,
            [
                ((local.shape[1], width), BF16),
                ((local.shape[1], width), BF16),
                ((height, NSUP * W), BF16),
                ((height, NSUP * W), BF16),
                ((height, width), F32),
            ],
            flops=1 << 32,
        )
        skip += len(order)
        got = moved(given, "c", 1)
        across = scattered(split_sum([kept, got], "y"), "y")
        cols = scattered(parts, "x")
        *across, first = tie(*across, total_of(cols))
        total = total_of(scattered(split_sum(across, "x"), "x"))
        keep = lax.dynamic_index_in_dim(first, at["zh"], 0, keepdims=False)
        give = lax.dynamic_index_in_dim(first, 1 - at["zh"], 0, keepdims=False)
        summed = -(keep + moved(give, "zh", 1))
        total, summed = tie(total, summed)
        columns.append(summed)
        total = total + sent(total, "zl", lambda a: a ^ 1)
        total = total + sent(total, "zl", lambda a: a ^ 2)
        total = total + moved(total, "zh", 1)
        parts = gathered(total, "x")
        total = kernel(functools.partial(join_kernel, "x"), parts, (4 * parts[0].shape[0], HALF))
        lanes = gathered(total, "y")
        finals += lanes + [moved(v, "c", 1) for v in lanes]

    pair_blocks, diagonal = kernel(
        functools.partial(final_kernel, orders),
        finals,
        [(len(PAIRS), W, W), (NSUP, W, W)],
        [((len(order) * W, W), F32) for order in orders],
    )
    wide = jnp.concatenate(columns, axis=1)
    columns = jnp.stack([wide[:, j * W : (j + 1) * W] for j in range(NSUP)])
    return (columns, pair_blocks, diagonal)


def solution(mesh):
    in_specs = (P(None, "col", None, "row"), P(None, BOTH, None), P(), P(), P(), P())
    out_specs = (P(None, BOTH, None), P(), P())
    return jax.shard_map(shards, mesh=mesh, in_specs=in_specs, out_specs=out_specs, check_vma=False)
```

```python
import functools

import jax
import jax.numpy as jnp
from jax import lax
from jax.experimental import pallas as pl
from jax.experimental.pallas import tpu as pltpu
from jax.sharding import PartitionSpec as P


W = 256
NSUP = 4
RW = 48
HALF = W // 2
SIZES = {"zh": 2, "x": 4, "y": 4, "zl": 4, "c": 2}
BOTH = ("row", "col")
CHUNKS = ((0, 1, 2, 3),)
F32, BF16 = jnp.float32, jnp.bfloat16
PAIRS = [(m, j) for j in range(NSUP) for m in range(j)]
ALL_BLOCKS = PAIRS + [(j, j) for j in range(NSUP)]
VMEM = pl.BlockSpec(memory_space=pltpu.VMEM)
SMEM = pl.BlockSpec(memory_space=pltpu.SMEM)


def place():
    row, col = lax.axis_index("row"), lax.axis_index("col")
    return {"zh": row >> 2, "x": row & 3, "y": col >> 3, "zl": (col >> 1) & 3, "c": col & 1}


def moved(value, axis, step):
    return sent(value, axis, lambda a: (a + step) % SIZES[axis])


def sent(value, axis, rule):
    names = list(SIZES)
    perm = []
    for device in range(256):
        rest, at = device, {}
        for name in reversed(names):
            at[name] = rest % SIZES[name]
            rest //= SIZES[name]
        at[axis] = rule(at[axis])
        target = 0
        for name in names:
            target = target * SIZES[name] + at[name]
        perm.append((device, target))
    return lax.ppermute(value, BOTH, perm)


def tie(*values):
    return lax.optimization_barrier(values)


def halves(value):
    top = value.astype(BF16)
    return top, (value - top.astype(F32)).astype(BF16)


def mul(left, right, over=(1, 0)):
    dims = (((over[0],), (over[1],)), ((), ()))
    dot = lambda u, v: lax.dot_general(u, v, dims, preferred_element_type=F32)
    return dot(left[0], right[0]) + (dot(left[1], right[0]) + dot(left[0], right[1]))


def couplings(couple, parent):
    linked = {}
    blocks = {}
    for j in range(NSUP):
        for m in range(j):
            now = parent[j] == m
            for p in range(m + 1, j):
                now = now | ((parent[j] == p) & linked[p, m])
            linked[j, m] = now
            blocks[j, m] = couple[j * (j - 1) // 2 + m] * jnp.where(now, 1.0, 0.0).astype(F32)
    return blocks


def pre_kernel(parent, pattern, factor, couple, out):
    first = (lax.axis_index("row") * 32 + lax.axis_index("col")) * RW
    block = first >> 8
    after = jnp.minimum(block + 1, pattern.shape[1] - 1)
    edge = (block + 1) * W - first
    low = lax.broadcasted_iota(jnp.int32, (RW, W), 0) < edge
    blocks = couplings(couple, parent)
    values = []
    for j in range(NSUP):
        here, there = pattern[j, block].astype(F32), pattern[j, after].astype(F32)
        values.append(factor[j] * jnp.where(low, here, there))
    for m in range(NSUP):
        out[:, m * W : (m + 1) * W] = values[m]
        left = halves(values[m])
        for j in range(m + 1, NSUP):
            values[j] = values[j] - mul(left, halves(blocks[j, m]))


def base_kernel(order, parent, couple, diag_inv, out, *held):
    chigh, clow, ihigh, ilow, shigh, slow = held
    at = lambda q, j: order.index((q, j))

    def keep(high, low, i, value):
        high[i], low[i] = halves(value)

    def kept(high, low, i):
        return high[i], low[i]

    for (j, m), value in couplings(couple, parent).items():
        keep(chigh, clow, at(m, j), value)
        keep(ihigh, ilow, at(m, j), -value)
    for gap in range(2, NSUP):
        for m in range(NSUP - gap):
            j = m + gap
            value = -(chigh[at(m, j)].astype(F32) + clow[at(m, j)].astype(F32))
            for q in range(m + 1, j):
                value = value - mul(kept(ihigh, ilow, at(m, q)), kept(chigh, clow, at(q, j)))
            keep(ihigh, ilow, at(m, j), value)
    for q in range(NSUP):
        out[at(q, q) * W : (at(q, q) + 1) * W, :] = diag_inv[q]
        keep(shigh, slow, at(q, q), diag_inv[q])
        for j in range(q + 1, NSUP):
            i = at(q, j)
            value = mul(kept(shigh, slow, at(q, q)), kept(ihigh, ilow, i))
            out[i * W : (i + 1) * W, :] = value
            keep(shigh, slow, i, value)
    for i, (m, j) in enumerate(order):
        rows = slice(i * W, (i + 1) * W)
        for q in range(m):
            out[rows, :] = out[rows, :] + mul(kept(ihigh, ilow, at(q, m)), kept(shigh, slow, at(q, j)), (0, 0))


def put(piece, top, bot, row_of):
    def step(i, carry):
        r = lax.div(i, 3)
        src = pl.multiple_of(i * 16, 16)
        dst = pl.multiple_of(row_of(r) + (i - 3 * r) * 16, 16)
        hi, lo = halves(piece[pl.ds(src, 16), :])
        top[pl.ds(dst, 16), :] = hi
        bot[pl.ds(dst, 16), :] = lo
        return carry

    lax.fori_loop(0, piece.shape[0] // 16, step, 0)


def put_columns(local, top, bot, blocks):
    span = local.shape[1] // 4
    for i, k in enumerate(blocks):
        src = pl.multiple_of(((place()["y"] - k) & 3) * span, 128)

        def step(t, carry, src=src, i=i):
            rows = pl.ds(pl.multiple_of(t * 16, 16), 16)
            hi, lo = halves(local[rows, pl.ds(src, span)])
            top[rows, i * span : (i + 1) * span] = hi
            bot[rows, i * span : (i + 1) * span] = lo
            return carry

        lax.fori_loop(0, local.shape[0] // 16, step, 0)


def early_kernel(local, *refs):
    pieces, out = refs[:6], refs[6]
    top, bot, ltop, lbot = refs[7:]
    at = place()
    put_columns(local, ltop, lbot, (0, 1, 3))
    for i, piece in enumerate(pieces):
        core = at["c"] ^ (i // 3)
        start = (i % 3) * 8
        put(piece, top, bot, lambda r: (start + ((at["zl"] - r) & 3) * 2 + core) * RW)
    out[...] = mul((ltop[...], lbot[...]), (top[...], bot[...]))


def main_kernel(chunk, order, skip, *refs):
    local, base, early = refs[:3]
    pieces, quads = refs[3:7], refs[7:11]
    outs = refs[11:15]
    kept, given = refs[15], refs[16]
    top, bot, ltop, lbot, rtop, rbot, result, ptop, pbot = refs[17:]
    at = place()
    put_columns(local, ltop, lbot, (2,))
    for i, piece in enumerate(pieces):
        core = at["c"] ^ (i // 2)
        start = 2 * (i % 2)
        put(piece, top, bot, lambda r: (((at["zl"] - r - start) & 3) * 2 + core) * RW)
    for k, piece in enumerate(quads):
        xa = (at["x"] - k) & 3
        for r in range(2):
            put(piece.at[r], rtop, rbot, lambda _: ((at["zh"] ^ r) * 4 + xa) * RW)
    result[...] = early[...] + mul((ltop[...], lbot[...]), (top[...], bot[...]))
    for k, out in enumerate(outs):
        xa = (at["x"] + k) & 3

        def step(t, carry, out=out, xa=xa):
            for r in range(2):
                src = pl.multiple_of((r * 4 + xa) * RW + t * 8, 8)
                out[r, pl.ds(pl.multiple_of(t * 8, 8), 8), :] = result[pl.ds(src, 8), :]
            return carry

        lax.fori_loop(0, RW // 8, step, 0)
    lead = (lax.axis_index("row") == 0) & (lax.axis_index("col") == 0)

    def part(t, carry):
        rows = pl.ds(pl.multiple_of(t * 16, 16), 16)
        hi, lo = halves(result[rows, :])
        ptop[rows, :] = hi
        pbot[rows, :] = lo
        return carry

    lax.fori_loop(0, result.shape[0] // 16, part, 0)
    cols = lambda s: (ptop[:, s * W : (s + 1) * W], pbot[:, s * W : (s + 1) * W])
    beside = lambda s: (rtop[:, s * W : (s + 1) * W], rbot[:, s * W : (s + 1) * W])
    even = at["c"] == 0
    for i, (m, j) in enumerate(order):
        if j in chunk:
            block = mul(beside(m), cols(chunk.index(j)), (0, 0))
        else:
            block = mul(cols(chunk.index(m)), beside(j), (0, 0))
        rows = slice(i * W, (i + 1) * W)
        block = block + jnp.where(lead, base[(skip + i) * W : (skip + i + 1) * W, :], 0.0)
        first, second = block[:, :HALF], block[:, HALF:]
        kept[rows, :] = jnp.where(even, first, second)
        given[rows, :] = jnp.where(even, second, first)


def join_kernel(axis, *refs):
    pieces, out = refs[:-1], refs[-1]
    at = place()[axis]
    rows = pieces[0].shape[0]
    for k, piece in enumerate(pieces):
        dst = pl.multiple_of(((at - k) & (SIZES[axis] - 1)) * rows, 8)
        out[pl.ds(dst, rows), :] = piece[...]


def add_split_kernel(axis, count, *refs):
    values, outs = refs[:count], refs[count:-1]
    whole = refs[-1]
    at = place()[axis]
    total = values[0][...]
    for value in values[1:]:
        total = total + value[...]
    whole[...] = total
    rows = outs[0].shape[0]
    for k, out in enumerate(outs):
        src = pl.multiple_of(((at + k) & (SIZES[axis] - 1)) * rows, 8)
        out[...] = whole[pl.ds(src, rows), :]


def final_kernel(orders, *refs):
    count = 8 * len(orders)
    pieces, pair_out, diag_out, wholes = refs[:count], refs[count], refs[count + 1], refs[count + 2 :]
    at = place()
    for i, order in enumerate(orders):
        whole = wholes[i]
        for par in range(2):
            for k in range(4):
                piece = pieces[i * 8 + par * 4 + k]
                rows = piece.shape[0]
                dst = pl.multiple_of(((at["y"] - k) & 3) * rows, 8)
                lane = pl.multiple_of((at["c"] ^ par) * HALF, HALF)
                whole[pl.ds(dst, rows), pl.ds(lane, HALF)] = piece[...]
        for b, (m, j) in enumerate(order):
            rows = slice(b * W, (b + 1) * W)
            if m == j:
                diag_out[j] = whole[rows, :]
            else:
                pair_out[PAIRS.index((m, j))] = whole[rows, :]


def kernel(body, args, out_shapes, scratch=(), smem=0, flops=0):
    single = not isinstance(out_shapes, list)
    return pl.pallas_call(
        body,
        out_shape=jax.ShapeDtypeStruct(out_shapes, F32)
        if single
        else [jax.ShapeDtypeStruct(s, F32) for s in out_shapes],
        in_specs=[SMEM] * smem + [VMEM] * (len(args) - smem),
        out_specs=VMEM if single else [VMEM] * len(out_shapes),
        scratch_shapes=[pltpu.VMEM(s, t) for s, t in scratch],
        compiler_params=pltpu.CompilerParams(vmem_limit_bytes=56 << 20),
        cost_estimate=pl.CostEstimate(
            flops=flops, transcendentals=0, bytes_accessed=sum(4 * a.size for a in args)
        ),
    )(*args)


def split_sum(values, axis):
    rows, width = values[0].shape
    n = SIZES[axis]
    return kernel(
        functools.partial(add_split_kernel, axis, len(values)),
        list(values),
        [(rows // n, width)] * n,
        [((rows, width), F32)],
    )


def scattered(pieces, axis):
    return [pieces[0]] + [moved(pieces[k], axis, k) for k in range(1, len(pieces))]


def gathered(value, axis):
    return [value] + [moved(value, axis, k) for k in range(1, SIZES[axis])]


def total_of(values):
    total = values[0]
    for value in values[1:]:
        total = total + value
    return total


def shards(inv_anc, factor_cols, couple, diag_inv, pattern, parent):
    at = place()
    local = inv_anc.reshape(-1, inv_anc.shape[3])
    height = local.shape[0]

    orders = []
    done = set()
    for chunk in CHUNKS:
        order = [b for b in ALL_BLOCKS if (b[0] in chunk or b[1] in chunk) and b not in done]
        done |= set(order)
        orders.append(order)

    own = kernel(
        pre_kernel, [parent, pattern, factor_cols, couple], (RW, NSUP * W), smem=2, flops=1 << 20
    )

    near = jnp.concatenate(gathered(own, "zl"), axis=0)
    near, later = tie(near, own)
    left, right = moved(near, "y", 1), moved(near, "y", 3)

    pair = jnp.stack([later, moved(later, "zh", 1)])
    pair, couple_later = tie(pair, couple)
    quads = gathered(pair, "x")

    (chunk,), (order,) = CHUNKS, orders
    base = kernel(
        functools.partial(base_kernel, order),
        [parent, couple_later, diag_inv],
        (len(order) * W, W),
        [((len(order), W, W), BF16)] * 6,
        smem=1,
        flops=1 << 31,
    )
    left, right, base = tie(left, right, base)
    half = near.shape[0] // 2
    far_a, far_b = moved(left[:half], "y", 1), moved(right[half:], "y", 3)
    mine = [near, left, right]
    pieces = mine + [moved(v, "c", 1) for v in mine]
    width = len(chunk) * W
    tall = len(order) * W
    span = local.shape[1] // 4
    early = kernel(
        early_kernel,
        [local] + pieces,
        (height, width),
        [((3 * span, width), BF16)] * 2 + [((height, 3 * span), BF16)] * 2,
        flops=1 << 32,
    )
    far_a, far_b, early = tie(far_a, far_b, early)
    columns = []
    finals = []
    skip = 0
    *parts, kept, given = kernel(
        functools.partial(main_kernel, chunk, order, skip),
        [local, base, early, far_a, far_b, moved(far_a, "c", 1), moved(far_b, "c", 1)] + quads,
        [(2, RW, width)] * 4 + [(tall, HALF)] * 2,
        [((span, width), BF16)] * 2
        + [((height, span), BF16)] * 2
        + [((height, NSUP * W), BF16)] * 2
        + [((height, width), F32)]
        + [((height, width), BF16)] * 2,
        flops=1 << 32,
    )
    got = moved(given, "c", 1)
    across = scattered(split_sum([kept, got], "y"), "y")
    cols = scattered(parts, "x")
    *across, first = tie(*across, total_of(cols))
    total = total_of(scattered(split_sum(across, "x"), "x"))
    total = total + sent(total, "zl", lambda a: a ^ 1)
    total = total + sent(total, "zl", lambda a: a ^ 2)
    total = total + moved(total, "zh", 1)
    total, first = tie(total, first)
    keep = lax.dynamic_index_in_dim(first, at["zh"], 0, keepdims=False)
    give = lax.dynamic_index_in_dim(first, 1 - at["zh"], 0, keepdims=False)
    columns.append(-(keep + moved(give, "zh", 1)))
    parts = gathered(total, "x")
    total = kernel(functools.partial(join_kernel, "x"), parts, (4 * parts[0].shape[0], HALF))
    lanes = gathered(total, "y")
    finals += lanes + [moved(v, "c", 1) for v in lanes]

    pair_blocks, diagonal = kernel(
        functools.partial(final_kernel, orders),
        finals,
        [(len(PAIRS), W, W), (NSUP, W, W)],
        [((len(order) * W, W), F32) for order in orders],
    )
    wide = jnp.concatenate(columns, axis=1)
    columns = jnp.stack([wide[:, j * W : (j + 1) * W] for j in range(NSUP)])
    return (columns, pair_blocks, diagonal)


def solution(mesh):
    in_specs = (P(None, "col", None, "row"), P(None, BOTH, None), P(), P(), P(), P())
    out_specs = (P(None, BOTH, None), P(), P())

    return jax.shard_map(shards, mesh=mesh, in_specs=in_specs, out_specs=out_specs, check_vma=False)
```

```python
import functools

import jax
import jax.numpy as jnp
from jax import lax
from jax.experimental import pallas as pl
from jax.experimental.pallas import tpu as pltpu
from jax.sharding import PartitionSpec as P


W = 256
NSUP = 4
RW = 48
HALF = W // 2
SIZES = {"zh": 2, "x": 4, "y": 4, "zl": 4, "c": 2}
BOTH = ("row", "col")
F32, BF16 = jnp.float32, jnp.bfloat16
PAIRS = [(m, j) for j in range(NSUP) for m in range(j)]
ALL_BLOCKS = PAIRS + [(j, j) for j in range(NSUP)]
VMEM = pl.BlockSpec(memory_space=pltpu.VMEM)
SMEM = pl.BlockSpec(memory_space=pltpu.SMEM)


def place():
    row, col = lax.axis_index("row"), lax.axis_index("col")
    return {"zh": row >> 2, "x": row & 3, "y": col >> 3, "zl": (col >> 1) & 3, "c": col & 1}


def moved(value, axis, step):
    return sent(value, axis, lambda a: (a + step) % SIZES[axis])


def sent(value, axis, rule):
    names = list(SIZES)
    perm = []
    for device in range(256):
        rest, at = device, {}
        for name in reversed(names):
            at[name] = rest % SIZES[name]
            rest //= SIZES[name]
        at[axis] = rule(at[axis])
        target = 0
        for name in names:
            target = target * SIZES[name] + at[name]
        perm.append((device, target))
    return lax.ppermute(value, BOTH, perm)


def tie(*values):
    return lax.optimization_barrier(values)


def halves(value):
    top = value.astype(BF16)
    return top, (value - top.astype(F32)).astype(BF16)


def mul(left, right, over=(1, 0)):
    dims = (((over[0],), (over[1],)), ((), ()))
    dot = lambda u, v: lax.dot_general(u, v, dims, preferred_element_type=F32)
    return dot(left[0], right[0]) + (dot(left[1], right[0]) + dot(left[0], right[1]))


def couplings(couple, parent):
    linked = {}
    blocks = {}
    for j in range(NSUP):
        for m in range(j):
            now = parent[j] == m
            for p in range(m + 1, j):
                now = now | ((parent[j] == p) & linked[p, m])
            linked[j, m] = now
            blocks[j, m] = couple[j * (j - 1) // 2 + m] * jnp.where(now, 1.0, 0.0).astype(F32)
    return blocks


def pre_kernel(parent, pattern, factor, couple, out):
    first = (lax.axis_index("row") * 32 + lax.axis_index("col")) * RW
    block = first >> 8
    after = jnp.minimum(block + 1, pattern.shape[1] - 1)
    edge = (block + 1) * W - first
    low = lax.broadcasted_iota(jnp.int32, (RW, W), 0) < edge
    blocks = couplings(couple, parent)
    values = []
    for j in range(NSUP):
        here, there = pattern[j, block].astype(F32), pattern[j, after].astype(F32)
        values.append(factor[j] * jnp.where(low, here, there))
    for m in range(NSUP):
        out[:, m * W : (m + 1) * W] = values[m]
        left = halves(values[m])
        for j in range(m + 1, NSUP):
            values[j] = values[j] - mul(left, halves(blocks[j, m]))


def base_kernel(order, parent, couple, diag_inv, out, *held):
    chigh, clow, ihigh, ilow, shigh, slow = held
    at = lambda q, j: order.index((q, j))

    def keep(high, low, i, value):
        high[i], low[i] = halves(value)

    def kept(high, low, i):
        return high[i], low[i]

    for (j, m), value in couplings(couple, parent).items():
        keep(chigh, clow, at(m, j), value)
        keep(ihigh, ilow, at(m, j), -value)
    for gap in range(2, NSUP):
        for m in range(NSUP - gap):
            j = m + gap
            value = -(chigh[at(m, j)].astype(F32) + clow[at(m, j)].astype(F32))
            for q in range(m + 1, j):
                value = value - mul(kept(ihigh, ilow, at(m, q)), kept(chigh, clow, at(q, j)))
            keep(ihigh, ilow, at(m, j), value)
    for q in range(NSUP):
        out[at(q, q) * W : (at(q, q) + 1) * W, :] = diag_inv[q]
        keep(shigh, slow, at(q, q), diag_inv[q])
        for j in range(q + 1, NSUP):
            i = at(q, j)
            value = mul(kept(shigh, slow, at(q, q)), kept(ihigh, ilow, i))
            out[i * W : (i + 1) * W, :] = value
            keep(shigh, slow, i, value)
    for i, (m, j) in enumerate(order):
        rows = slice(i * W, (i + 1) * W)
        for q in range(m):
            out[rows, :] = out[rows, :] + mul(kept(ihigh, ilow, at(q, m)), kept(shigh, slow, at(q, j)), (0, 0))


def put(piece, top, bot, row_of):
    def step(r, carry):
        src = pl.multiple_of(r * RW, 16)
        dst = pl.multiple_of(row_of(r), 16)
        hi, lo = halves(piece[pl.ds(src, RW), :])
        top[pl.ds(dst, RW), :] = hi
        bot[pl.ds(dst, RW), :] = lo
        return carry

    lax.fori_loop(0, piece.shape[0] // RW, step, 0)


def near_kernel(local, near, twin, cross, out, ltop, lbot, rtop, rbot, top, bot):
    at = place()
    span = local.shape[1] // 4
    for i, k in enumerate((0, 1, 3, 2)):
        src = pl.multiple_of(((at["y"] - k) & 3) * span, 128)

        def step(t, carry, src=src, i=i):
            rows = pl.ds(pl.multiple_of(t * RW, 16), RW)
            hi, lo = halves(local[rows, pl.ds(src, span)])
            ltop[rows, i * span : (i + 1) * span] = hi
            lbot[rows, i * span : (i + 1) * span] = lo
            return carry

        lax.fori_loop(0, local.shape[0] // RW, step, 0)
    put(cross, rtop, rbot, lambda r: ((at["x"] - r) & 3) * RW)
    for par, piece in enumerate((near, twin)):
        core = at["c"] ^ par
        put(piece, top, bot, lambda r: (((at["zl"] - r) & 3) * 2 + core) * RW)
    out[...] = mul((ltop[:, :span], lbot[:, :span]), (top[...], bot[...]))


def early_kernel(start, ltop, lbot, left, right, ltwin, rtwin, out, top, bot):
    at = place()
    span = ltop.shape[1] // 4
    for i, piece in enumerate((left, right, ltwin, rtwin)):
        core = at["c"] ^ (i // 2)
        put(piece, top, bot, lambda r: ((i % 2) * 8 + ((at["zl"] - r) & 3) * 2 + core) * RW)
    cols = slice(span, 3 * span)
    out[...] = start[...] + mul((ltop[:, cols], lbot[:, cols]), (top[...], bot[...]))


def main_kernel(order, *refs):
    early, base, ltop, lbot, ra, rb, distant = refs[:7]
    pieces, outs = refs[7:11], refs[11:15]
    kept, given = refs[15], refs[16]
    top, bot, rtop, rbot, result, ptop, pbot = refs[17:]
    at = place()
    span = ltop.shape[1] // 4
    quad = ra.shape[0]
    for i, piece in enumerate(pieces):
        core = at["c"] ^ (i // 2)
        start = 2 * (i % 2)
        put(piece, top, bot, lambda r: (((at["zl"] - r - start) & 3) * 2 + core) * RW)
    here = pl.ds(pl.multiple_of(at["zh"] * quad, 16), quad)
    rtop[here, :] = ra[...]
    rbot[here, :] = rb[...]
    put(distant, rtop, rbot, lambda r: (1 - at["zh"]) * quad + ((at["x"] - r) & 3) * RW)
    cols = slice(3 * span, 4 * span)
    value = early[...] + mul((ltop[:, cols], lbot[:, cols]), (top[...], bot[...]))
    result[...] = value
    hi, lo = halves(value)
    ptop[...] = hi
    pbot[...] = lo
    for k, out in enumerate(outs):
        xa = (at["x"] + k) & 3
        for r in range(2):
            out[r] = result[pl.ds(pl.multiple_of((r * 4 + xa) * RW, 16), RW), :]
    lead = (lax.axis_index("row") == 0) & (lax.axis_index("col") == 0)
    even = at["c"] == 0
    for i, (m, j) in enumerate(order):
        one, two = slice(m * W, (m + 1) * W), slice(j * W, (j + 1) * W)
        block = mul((rtop[:, one], rbot[:, one]), (ptop[:, two], pbot[:, two]), (0, 0))
        rows = slice(i * W, (i + 1) * W)
        block = block + jnp.where(lead, base[rows, :], 0.0)
        first, second = block[:, :HALF], block[:, HALF:]
        kept[rows, :] = jnp.where(even, first, second)
        given[rows, :] = jnp.where(even, second, first)


def pick_kernel(*refs):
    pieces, keep, give = refs[:4], refs[4], refs[5]
    zh = place()["zh"]
    for out, side in ((keep, zh), (give, 1 - zh)):
        total = pieces[0][side]
        for piece in pieces[1:]:
            total = total + piece[side]
        out[...] = total


def columns_kernel(keep, got, out):
    for j in range(NSUP):
        cols = slice(j * W, (j + 1) * W)
        out[j] = -(keep[:, cols] + got[:, cols])


def join_kernel(axis, *refs):
    pieces, out = refs[:-1], refs[-1]
    at = place()[axis]
    rows = pieces[0].shape[0]
    for k, piece in enumerate(pieces):
        dst = pl.multiple_of(((at - k) & (SIZES[axis] - 1)) * rows, 8)
        out[pl.ds(dst, rows), :] = piece[...]


def add_split_kernel(axis, count, *refs):
    values, outs = refs[:count], refs[count:]
    at = place()[axis]
    rows = outs[0].shape[0]
    for k, out in enumerate(outs):
        src = pl.ds(pl.multiple_of(((at + k) & (SIZES[axis] - 1)) * rows, 8), rows)
        total = values[0][src, :]
        for value in values[1:]:
            total = total + value[src, :]
        out[...] = total


def final_kernel(orders, *refs):
    count = 8 * len(orders)
    pieces, pair_out, diag_out, wholes = refs[:count], refs[count], refs[count + 1], refs[count + 2 :]
    at = place()
    for i, order in enumerate(orders):
        whole = wholes[i]
        for par in range(2):
            for k in range(4):
                piece = pieces[i * 8 + par * 4 + k]
                rows = piece.shape[0]
                dst = pl.multiple_of(((at["y"] - k) & 3) * rows, 8)
                lane = pl.multiple_of((at["c"] ^ par) * HALF, HALF)
                whole[pl.ds(dst, rows), pl.ds(lane, HALF)] = piece[...]
        for b, (m, j) in enumerate(order):
            rows = slice(b * W, (b + 1) * W)
            if m == j:
                diag_out[j] = whole[rows, :]
            else:
                pair_out[PAIRS.index((m, j))] = whole[rows, :]


def kernel(body, args, out_shapes, scratch=(), smem=0, flops=0):
    single = not isinstance(out_shapes, list)
    return pl.pallas_call(
        body,
        out_shape=jax.ShapeDtypeStruct(out_shapes, F32)
        if single
        else [jax.ShapeDtypeStruct(s, F32) if isinstance(s[-1], int) else jax.ShapeDtypeStruct(*s) for s in out_shapes],
        in_specs=[SMEM] * smem + [VMEM] * (len(args) - smem),
        out_specs=VMEM if single else [VMEM] * len(out_shapes),
        scratch_shapes=[pltpu.VMEM(s, t) for s, t in scratch],
        compiler_params=pltpu.CompilerParams(vmem_limit_bytes=56 << 20),
        cost_estimate=pl.CostEstimate(
            flops=flops, transcendentals=0, bytes_accessed=sum(4 * a.size for a in args)
        ),
    )(*args)


def split_sum(values, axis):
    rows, width = values[0].shape
    n = SIZES[axis]
    return kernel(
        functools.partial(add_split_kernel, axis, len(values)),
        list(values),
        [(rows // n, width)] * n,
    )


def scattered(pieces, axis):
    return [pieces[0]] + [moved(pieces[k], axis, k) for k in range(1, len(pieces))]


def gathered(value, axis):
    return [value] + [moved(value, axis, k) for k in range(1, SIZES[axis])]


def total_of(values):
    total = values[0]
    for value in values[1:]:
        total = total + value
    return total


def shards(inv_anc, factor_cols, couple, diag_inv, pattern, parent):
    local = inv_anc.reshape(-1, inv_anc.shape[3])
    height = local.shape[0]

    own = kernel(
        pre_kernel, [parent, pattern, factor_cols, couple], (RW, NSUP * W), smem=2, flops=1 << 20
    )
    width = NSUP * W
    tall = len(ALL_BLOCKS) * W
    span = local.shape[1] // 4

    near = gathered(own, "zl")
    cross = gathered(own, "x")
    _, couple_later = tie(own, couple)
    base = kernel(
        functools.partial(base_kernel, ALL_BLOCKS),
        [parent, couple_later, diag_inv],
        (tall, W),
        [((len(ALL_BLOCKS), W, W), BF16)] * 6,
        smem=1,
        flops=1 << 31,
    )
    near = jnp.concatenate(near, axis=0)
    near, base, *cross = tie(near, base, *cross)
    cross = jnp.concatenate(cross, axis=0)

    left, right = moved(near, "y", 1), moved(near, "y", 3)
    distant = moved(cross, "zh", 1)
    start, ltop, lbot, ra, rb = kernel(
        near_kernel,
        [local, near, moved(near, "c", 1), cross],
        [(height, width)] + [((height, 4 * span), BF16)] * 2 + [(cross.shape, BF16)] * 2,
        [((span, width), BF16)] * 2,
        flops=1 << 31,
    )
    left, right, start = tie(left, right, start)
    half = near.shape[0] // 2
    far_a, far_b = moved(left[:half], "y", 1), moved(right[half:], "y", 3)
    early = kernel(
        early_kernel,
        [start, ltop, lbot, left, right, moved(left, "c", 1), moved(right, "c", 1)],
        (height, width),
        [((2 * span, width), BF16)] * 2,
        flops=1 << 31,
    )
    far_a, far_b, early = tie(far_a, far_b, early)
    *parts, kept, given = kernel(
        functools.partial(main_kernel, ALL_BLOCKS),
        [early, base, ltop, lbot, ra, rb, distant]
        + [far_a, far_b, moved(far_a, "c", 1), moved(far_b, "c", 1)],
        [(2, RW, width)] * 4 + [(tall, HALF)] * 2,
        [((span, width), BF16)] * 2
        + [((height, width), BF16)] * 2
        + [((height, width), F32)]
        + [((height, width), BF16)] * 2,
        flops=1 << 32,
    )

    got = moved(given, "c", 1)
    cut = split_sum([kept, got], "y")
    cols = scattered(parts, "x")
    across = scattered(cut, "y")
    keep, give = kernel(pick_kernel, cols, [(RW, width)] * 2)
    summed = moved(give, "zh", 1)
    cut = split_sum(across, "x")
    total = total_of(scattered(cut, "x"))
    total, summed = tie(total, summed)
    total = total + sent(total, "zl", lambda a: a ^ 1)
    total = total + sent(total, "zl", lambda a: a ^ 2)
    total = total + moved(total, "zh", 1)
    lines = gathered(total, "x")
    total = kernel(functools.partial(join_kernel, "x"), lines, (4 * total.shape[0], HALF))
    lanes = gathered(total, "y")
    pair_blocks, diagonal = kernel(
        functools.partial(final_kernel, [ALL_BLOCKS]),
        lanes + [moved(v, "c", 1) for v in lanes],
        [(len(PAIRS), W, W), (NSUP, W, W)],
        [((tall, W), F32)],
    )
    columns = kernel(columns_kernel, [keep, summed], (NSUP, RW, W))
    return (columns, pair_blocks, diagonal)


def solution(mesh):
    in_specs = (P(None, "col", None, "row"), P(None, BOTH, None), P(), P(), P(), P())
    out_specs = (P(None, BOTH, None), P(), P())

    return jax.shard_map(shards, mesh=mesh, in_specs=in_specs, out_specs=out_specs, check_vma=False)
```

```python
import functools

import jax
import jax.numpy as jnp
from jax import lax
from jax.experimental import pallas as pl
from jax.experimental.pallas import tpu as pltpu
from jax.sharding import PartitionSpec as P


W = 256
NSUP = 4
RW = 48
SIZES = {"zh": 2, "x": 4, "y": 4, "zl": 4, "c": 2}
BOTH = ("row", "col")
F32, BF16 = jnp.float32, jnp.bfloat16
PAIRS = [(m, j) for j in range(NSUP) for m in range(j)]
BLOCKS = ([(0, 1), (0, 2), (1, 2), (0, 0), (1, 1)], [(0, 3), (1, 3), (2, 3), (2, 2), (3, 3)])
FACTORS = ([(0, 5), (4, 2), (5, 2), (0, 4), (1, 5)], [(0, 5), (1, 5), (2, 5), (2, 4), (3, 5)])
ALL_BLOCKS = BLOCKS[0] + BLOCKS[1]
VMEM = pl.BlockSpec(memory_space=pltpu.VMEM)
SMEM = pl.BlockSpec(memory_space=pltpu.SMEM)


def place():
    row, col = lax.axis_index("row"), lax.axis_index("col")
    return {"zh": row >> 2, "x": row & 3, "y": col >> 3, "zl": (col >> 1) & 3, "c": col & 1}


def moved(value, axis, step):
    return sent(value, axis, lambda a: (a + step) % SIZES[axis])


def sent(value, axis, rule):
    names = list(SIZES)
    perm = []
    for device in range(256):
        rest, at = device, {}
        for name in reversed(names):
            at[name] = rest % SIZES[name]
            rest //= SIZES[name]
        at[axis] = rule(at[axis])
        target = 0
        for name in names:
            target = target * SIZES[name] + at[name]
        perm.append((device, target))
    return lax.ppermute(value, BOTH, perm)


def tie(*values):
    return lax.optimization_barrier(values)


def halves(value):
    top = value.astype(BF16)
    return top, (value - top.astype(F32)).astype(BF16)


def mul(left, right, over=(1, 0)):
    dims = (((over[0],), (over[1],)), ((), ()))
    dot = lambda u, v: lax.dot_general(u, v, dims, preferred_element_type=F32)
    return dot(left[0], right[0]) + (dot(left[1], right[0]) + dot(left[0], right[1]))


def couplings(couple, parent):
    linked = {}
    blocks = {}
    for j in range(NSUP):
        for m in range(j):
            now = parent[j] == m
            for p in range(m + 1, j):
                now = now | ((parent[j] == p) & linked[p, m])
            linked[j, m] = now
            blocks[j, m] = couple[j * (j - 1) // 2 + m] * jnp.where(now, 1.0, 0.0).astype(F32)
    return blocks


def pre_kernel(parent, pattern, factor, couple, out):
    first = (lax.axis_index("row") * 32 + lax.axis_index("col")) * RW
    block = first >> 8
    after = jnp.minimum(block + 1, pattern.shape[1] - 1)
    edge = (block + 1) * W - first
    low = lax.broadcasted_iota(jnp.int32, (RW, W), 0) < edge
    blocks = couplings(couple, parent)
    values = []
    for j in range(NSUP):
        here, there = pattern[j, block].astype(F32), pattern[j, after].astype(F32)
        values.append(factor[j] * jnp.where(low, here, there))
    for m in range(NSUP):
        out[:, m * W : (m + 1) * W] = values[m]
        left = halves(values[m])
        for j in range(m + 1, NSUP):
            values[j] = values[j] - mul(left, halves(blocks[j, m]))


def base_tables(order):
    at = lambda q, j: order.index((q, j))
    rows = [(at(q, j), at(q, q), at(q, j)) for q in range(NSUP) for j in range(q + 1, NSUP)]
    split = len(rows)
    rows += [(at(m, j), at(q, m), at(q, j)) for j in range(NSUP) for m in range(j + 1) for q in range(m)]
    return split, rows


def base_kernel(order, parent, table, couple, diag_inv, out, *held):
    chigh, clow, ihigh, ilow, shigh, slow = held
    at = lambda q, j: order.index((q, j))

    def keep(high, low, i, value):
        high[i], low[i] = halves(value)

    def kept(high, low, i):
        return high[i], low[i]

    for (j, m), value in couplings(couple, parent).items():
        keep(chigh, clow, at(m, j), value)
        keep(ihigh, ilow, at(m, j), -value)
    for gap in range(2, NSUP):
        for m in range(NSUP - gap):
            j = m + gap
            value = -(chigh[at(m, j)].astype(F32) + clow[at(m, j)].astype(F32))
            for q in range(m + 1, j):
                value = value - mul(kept(ihigh, ilow, at(m, q)), kept(chigh, clow, at(q, j)))
            keep(ihigh, ilow, at(m, j), value)
    for q in range(NSUP):
        out[at(q, q) * W : (at(q, q) + 1) * W, :] = diag_inv[q]
        keep(shigh, slow, at(q, q), diag_inv[q])
    split, rows = base_tables(order)

    def scale(t, carry):
        i = table[t, 0]
        value = mul(kept(shigh, slow, table[t, 1]), kept(ihigh, ilow, table[t, 2]))
        out[pl.ds(pl.multiple_of(i * W, W), W), :] = value
        keep(shigh, slow, i, value)
        return carry

    def gain(t, carry):
        where = pl.ds(pl.multiple_of(table[t, 0] * W, W), W)
        left, right = kept(ihigh, ilow, table[t, 1]), kept(shigh, slow, table[t, 2])
        out[where, :] = out[where, :] + mul(left, right, (0, 0))
        return carry

    lax.fori_loop(0, split, scale, 0)
    lax.fori_loop(split, len(rows), gain, 0)


def put(piece, top, bot, row_of):
    def step(r, carry):
        src = pl.multiple_of(r * RW, 16)
        dst = pl.multiple_of(row_of(r), 16)
        hi, lo = halves(piece[pl.ds(src, RW), :])
        top[pl.ds(dst, RW), :] = hi
        bot[pl.ds(dst, RW), :] = lo
        return carry

    lax.fori_loop(0, piece.shape[0] // RW, step, 0)


def near_kernel(local, near, twin, cross, out, ltop, lbot, rtop, rbot, top, bot):
    at = place()
    span = local.shape[1] // 4
    for i, k in enumerate((0, 1, 3, 2)):
        src = pl.multiple_of(((at["y"] - k) & 3) * span, 128)

        def step(t, carry, src=src, i=i):
            rows = pl.ds(pl.multiple_of(t * RW, 16), RW)
            hi, lo = halves(local[rows, pl.ds(src, span)])
            ltop[rows, i * span : (i + 1) * span] = hi
            lbot[rows, i * span : (i + 1) * span] = lo
            return carry

        lax.fori_loop(0, local.shape[0] // RW, step, 0)
    put(cross, rtop, rbot, lambda r: ((at["x"] - r) & 3) * RW)
    for par, piece in enumerate((near, twin)):
        core = at["c"] ^ par
        put(piece, top, bot, lambda r: (((at["zl"] - r) & 3) * 2 + core) * RW)
    out[...] = mul((ltop[:, :span], lbot[:, :span]), (top[...], bot[...]))


def early_kernel(start, ltop, lbot, left, right, ltwin, rtwin, out, top, bot):
    at = place()
    span = ltop.shape[1] // 4
    for i, piece in enumerate((left, right, ltwin, rtwin)):
        core = at["c"] ^ (i // 2)
        put(piece, top, bot, lambda r: ((i % 2) * 8 + ((at["zl"] - r) & 3) * 2 + core) * RW)
    cols = slice(span, 3 * span)
    out[...] = start[...] + mul((ltop[:, cols], lbot[:, cols]), (top[...], bot[...]))


def late_kernel(*refs):
    early, ltop, lbot = refs[:3]
    pieces, outs = refs[3:7], refs[7:11]
    high, low, give = refs[11:14]
    top, bot, result = refs[14:]
    at = place()
    span = ltop.shape[1] // 4
    for i, piece in enumerate(pieces):
        core = at["c"] ^ (i // 2)
        start = 2 * (i % 2)
        put(piece, top, bot, lambda r: (((at["zl"] - r - start) & 3) * 2 + core) * RW)
    cols = slice(3 * span, 4 * span)
    result[...] = early[...] + mul((ltop[:, cols], lbot[:, cols]), (top[...], bot[...]))
    wide = give.shape[1]
    high[...], low[...] = halves(result[:, pl.ds(pl.multiple_of(at["c"] * wide, wide), wide)])
    give[...] = result[:, pl.ds(pl.multiple_of((1 - at["c"]) * wide, wide), wide)]
    for k, out in enumerate(outs):
        xa = (at["x"] + k) & 3
        for r in range(2):
            out[r] = result[pl.ds(pl.multiple_of((r * 4 + xa) * RW, 16), RW), :]


def window_blocks(top, bot, core):
    for first, second in zip(*FACTORS):
        left, right = [
            pl.ds(pl.multiple_of(jnp.where(core == 0, first[side], second[side]) * W, W), W) for side in (0, 1)
        ]
        yield mul((top[:, left], bot[:, left]), (top[:, right], bot[:, right]), (0, 0))


def own_kernel(high, low, ra, rb, distant, cross2, distant2, out, rtop, rbot, top, bot):
    at = place()
    quad = ra.shape[0]
    wide = NSUP * W
    here = pl.ds(pl.multiple_of(at["zh"] * quad, 16), quad)
    top[here, :wide] = ra[...]
    bot[here, :wide] = rb[...]
    put(distant, top.at[:, :wide], bot.at[:, :wide], lambda r: (1 - at["zh"]) * quad + ((at["x"] - r) & 3) * RW)
    top[:, wide:] = high[...]
    bot[:, wide:] = low[...]
    for i, block in enumerate(window_blocks(top, bot, at["c"])):
        out[i * W : (i + 1) * W, :] = block
    for side, piece in ((at["zh"], cross2), (1 - at["zh"], distant2)):
        put(piece, rtop, rbot, lambda r: side * quad + ((at["x"] - r) & 3) * RW)


def twin_kernel(own, rtop, rbot, got, base, *refs):
    outs, (top, bot, whole) = refs[:4], refs[4:]
    at = place()
    wide = NSUP * W
    top[:, :wide] = rtop[...]
    bot[:, :wide] = rbot[...]
    top[:, wide:], bot[:, wide:] = halves(got[...])
    lead = (lax.axis_index("row") == 0) & (lax.axis_index("col") < 2)
    for i, block in enumerate(window_blocks(top, bot, at["c"])):
        rows = slice(i * W, (i + 1) * W)
        plus = base[pl.ds(pl.multiple_of(at["c"] * own.shape[0] + i * W, W), W), :]
        whole[rows, :] = own[rows, :] + block + jnp.where(lead, plus, 0.0)
    size = outs[0].shape[0]
    for k, out in enumerate(outs):
        out[...] = whole[pl.ds(pl.multiple_of(((at["y"] + k) & 3) * size, 8), size), :]


def pick_kernel(*refs):
    pieces, keep, give = refs[:4], refs[4], refs[5]
    zh = place()["zh"]
    for out, side in ((keep, zh), (give, 1 - zh)):
        total = pieces[0][side]
        for piece in pieces[1:]:
            total = total + piece[side]
        out[...] = total


def columns_kernel(keep, got, out):
    for j in range(NSUP):
        cols = slice(j * W, (j + 1) * W)
        out[j] = -(keep[:, cols] + got[:, cols])


def join_kernel(axis, *refs):
    pieces, out = refs[:-1], refs[-1]
    at = place()[axis]
    rows = pieces[0].shape[0]
    for k, piece in enumerate(pieces):
        dst = pl.multiple_of(((at - k) & (SIZES[axis] - 1)) * rows, 8)
        out[pl.ds(dst, rows), :] = piece[...]


def add_split_kernel(axis, count, *refs):
    values, outs = refs[:count], refs[count:]
    at = place()[axis]
    rows = outs[0].shape[0]
    for k, out in enumerate(outs):
        src = pl.ds(pl.multiple_of(((at + k) & (SIZES[axis] - 1)) * rows, 8), rows)
        total = values[0][src, :]
        for value in values[1:]:
            total = total + value[src, :]
        out[...] = total


def final_kernel(*refs):
    pieces, pair_out, diag_out, whole = refs[:8], refs[8], refs[9], refs[10]
    at = place()
    rows = pieces[0].shape[0]
    for par in range(2):
        core = at["c"] ^ par
        for k in range(4):
            dst = pl.multiple_of(((at["y"] - k) & 3) * rows, 8)
            whole[pl.ds(dst, rows), :] = pieces[par * 4 + k][...]
        for i in range(3):
            pair_out[core * 3 + i] = whole[i * W : (i + 1) * W, :]
        for i in range(2):
            diag_out[core * 2 + i] = whole[(3 + i) * W : (4 + i) * W, :]


def kernel(body, args, out_shapes, scratch=(), smem=0, flops=0):
    single = not isinstance(out_shapes, list)
    return pl.pallas_call(
        body,
        out_shape=jax.ShapeDtypeStruct(out_shapes, F32)
        if single
        else [jax.ShapeDtypeStruct(s, F32) if isinstance(s[-1], int) else jax.ShapeDtypeStruct(*s) for s in out_shapes],
        in_specs=[SMEM] * smem + [VMEM] * (len(args) - smem),
        out_specs=VMEM if single else [VMEM] * len(out_shapes),
        scratch_shapes=[pltpu.VMEM(s, t) for s, t in scratch],
        compiler_params=pltpu.CompilerParams(vmem_limit_bytes=56 << 20),
        cost_estimate=pl.CostEstimate(
            flops=flops, transcendentals=0, bytes_accessed=sum(4 * a.size for a in args)
        ),
    )(*args)


def split_sum(values, axis):
    rows, width = values[0].shape
    n = SIZES[axis]
    return kernel(
        functools.partial(add_split_kernel, axis, len(values)),
        list(values),
        [(rows // n, width)] * n,
    )


def scattered(pieces, axis):
    return [pieces[0]] + [moved(pieces[k], axis, k) for k in range(1, len(pieces))]


def gathered(value, axis):
    return [value] + [moved(value, axis, k) for k in range(1, SIZES[axis])]


def total_of(values):
    total = values[0]
    for value in values[1:]:
        total = total + value
    return total


def shards(inv_anc, factor_cols, couple, diag_inv, pattern, parent):
    local = inv_anc.reshape(-1, inv_anc.shape[3])
    height = local.shape[0]

    own = kernel(
        pre_kernel, [parent, pattern, factor_cols, couple], (RW, NSUP * W), smem=2, flops=1 << 20
    )
    width = NSUP * W
    tall = len(ALL_BLOCKS) * W
    span = local.shape[1] // 4

    near = gathered(own, "zl")
    cross = gathered(own, "x")
    _, couple_later = tie(own, couple)
    table = jnp.array(base_tables(ALL_BLOCKS)[1], jnp.int32)
    base = kernel(
        functools.partial(base_kernel, ALL_BLOCKS),
        [parent, table, couple_later, diag_inv],
        (tall, W),
        [((len(ALL_BLOCKS), W, W), BF16)] * 6,
        smem=2,
        flops=1 << 31,
    )
    near = jnp.concatenate(near, axis=0)
    near, base, *cross = tie(near, base, *cross)
    cross = jnp.concatenate(cross, axis=0)

    left, right = moved(near, "y", 1), moved(near, "y", 3)
    distant = moved(cross, "zh", 1)
    cross2 = moved(cross, "c", 1)
    start, ltop, lbot, ra, rb = kernel(
        near_kernel,
        [local, near, moved(near, "c", 1), cross],
        [(height, width)] + [((height, 4 * span), BF16)] * 2 + [(cross.shape, BF16)] * 2,
        [((span, width), BF16)] * 2,
        flops=1 << 31,
    )
    left, right, start = tie(left, right, start)
    half = near.shape[0] // 2
    far_a, far_b = moved(left[:half], "y", 1), moved(right[half:], "y", 3)
    early = kernel(
        early_kernel,
        [start, ltop, lbot, left, right, moved(left, "c", 1), moved(right, "c", 1)],
        (height, width),
        [((2 * span, width), BF16)] * 2,
        flops=1 << 31,
    )
    far_a, far_b, early = tie(far_a, far_b, early)
    *parts, high, low, give = kernel(
        late_kernel,
        [early, ltop, lbot, far_a, far_b, moved(far_a, "c", 1), moved(far_b, "c", 1)],
        [(2, RW, width)] * 4 + [((height, width // 2), BF16)] * 2 + [(height, width // 2)],
        [((span, width), BF16)] * 2 + [((height, width), F32)],
        flops=1 << 31,
    )

    got = moved(give, "c", 1)
    sums, rtop, rbot = kernel(
        own_kernel,
        [high, low, ra, rb, distant, cross2, moved(distant, "c", 1)],
        [(tall // 2, W)] + [((height, width), BF16)] * 2,
        [((height, width + width // 2), BF16)] * 2,
        flops=1 << 31,
    )
    cut = kernel(
        twin_kernel,
        [sums, rtop, rbot, got, base],
        [(tall // 8, W)] * 4,
        [((height, width + width // 2), BF16)] * 2 + [((tall // 2, W), F32)],
        flops=1 << 31,
    )
    across = scattered(cut, "y")
    cols = scattered(parts, "x")
    keep, give = kernel(pick_kernel, cols, [(RW, width)] * 2)
    summed = moved(give, "zh", 1)
    cut = split_sum(across, "x")
    total = total_of(scattered(cut, "x"))
    total = total + sent(total, "zl", lambda a: a ^ 1)
    total = total + sent(total, "zl", lambda a: a ^ 2)
    total = total + moved(total, "zh", 1)
    lines = gathered(total, "x")
    total = kernel(functools.partial(join_kernel, "x"), lines, (4 * total.shape[0], W))
    lanes = gathered(total, "y")
    twins = [moved(v, "c", 1) for v in lanes]
    pair_blocks, diagonal = kernel(
        final_kernel,
        lanes + twins,
        [(len(PAIRS), W, W), (NSUP, W, W)],
        [((tall // 2, W), F32)],
    )
    keep, pair_blocks, diagonal = tie(keep, pair_blocks, diagonal)
    columns = kernel(columns_kernel, [keep, summed], (NSUP, RW, W))
    return (columns, pair_blocks, diagonal)


def solution(mesh):
    in_specs = (P(None, "col", None, "row"), P(None, BOTH, None), P(), P(), P(), P())
    out_specs = (P(None, BOTH, None), P(), P())

    return jax.shard_map(shards, mesh=mesh, in_specs=in_specs, out_specs=out_specs, check_vma=False)
```

```python
import functools

import jax
import jax.numpy as jnp
from jax import lax
from jax.experimental import pallas as pl
from jax.experimental.pallas import tpu as pltpu
from jax.sharding import PartitionSpec as P


W = 256
NSUP = 4
RW = 48
SIZES = {"zh": 2, "x": 4, "y": 4, "zl": 4, "c": 2}
BOTH = ("row", "col")
F32, BF16 = jnp.float32, jnp.bfloat16
PAIRS = [(m, j) for j in range(NSUP) for m in range(j)]
BLOCKS = ([(0, 1), (2, 0), (2, 1), (0, 0), (1, 1)], [(0, 3), (1, 3), (2, 3), (2, 2), (3, 3)])
ALL_BLOCKS = [tuple(sorted(b)) for b in BLOCKS[0] + BLOCKS[1]]
TURNED = (1, 2)
VMEM = pl.BlockSpec(memory_space=pltpu.VMEM)
SMEM = pl.BlockSpec(memory_space=pltpu.SMEM)


def place():
    row, col = lax.axis_index("row"), lax.axis_index("col")
    return {"zh": row >> 2, "x": row & 3, "y": col >> 3, "zl": (col >> 1) & 3, "c": col & 1}


def moved(value, axis, step):
    return sent(value, axis, lambda a: (a + step) % SIZES[axis])


def sent(value, axis, rule):
    names = list(SIZES)
    perm = []
    for device in range(256):
        rest, at = device, {}
        for name in reversed(names):
            at[name] = rest % SIZES[name]
            rest //= SIZES[name]
        at[axis] = rule(at[axis])
        target = 0
        for name in names:
            target = target * SIZES[name] + at[name]
        perm.append((device, target))
    return lax.ppermute(value, BOTH, perm)


def tie(*values):
    return lax.optimization_barrier(values)


def halves(value):
    top = value.astype(BF16)
    return top, (value - top.astype(F32)).astype(BF16)


def mul(left, right, over=(1, 0)):
    dims = (((over[0],), (over[1],)), ((), ()))
    dot = lambda u, v: lax.dot_general(u, v, dims, preferred_element_type=F32)
    return dot(left[0], right[0]) + (dot(left[1], right[0]) + dot(left[0], right[1]))


def couplings(couple, parent):
    linked = {}
    blocks = {}
    for j in range(NSUP):
        for m in range(j):
            now = parent[j] == m
            for p in range(m + 1, j):
                now = now | ((parent[j] == p) & linked[p, m])
            linked[j, m] = now
            blocks[j, m] = couple[j * (j - 1) // 2 + m] * jnp.where(now, 1.0, 0.0).astype(F32)
    return blocks


def pre_kernel(parent, pattern, factor, couple, out):
    first = (lax.axis_index("row") * 32 + lax.axis_index("col")) * RW
    block = first >> 8
    after = jnp.minimum(block + 1, pattern.shape[1] - 1)
    edge = (block + 1) * W - first
    low = lax.broadcasted_iota(jnp.int32, (RW, W), 0) < edge
    blocks = couplings(couple, parent)
    values = []
    for j in range(NSUP):
        here, there = pattern[j, block].astype(F32), pattern[j, after].astype(F32)
        values.append(factor[j] * jnp.where(low, here, there))
    for m in range(NSUP):
        out[:, m * W : (m + 1) * W] = values[m]
        left = halves(values[m])
        for j in range(m + 1, NSUP):
            values[j] = values[j] - mul(left, halves(blocks[j, m]))


def base_tables(order):
    at = lambda q, j: order.index((q, j))
    rows = [(at(q, j), at(q, q), at(q, j)) for q in range(NSUP) for j in range(q + 1, NSUP)]
    split = len(rows)
    rows += [(at(m, j), at(q, m), at(q, j)) for j in range(NSUP) for m in range(j + 1) for q in range(m)]
    return split, rows


def base_kernel(order, parent, table, couple, diag_inv, out, *held):
    chigh, clow, ihigh, ilow, shigh, slow = held
    at = lambda q, j: order.index((q, j))

    def keep(high, low, i, value):
        high[i], low[i] = halves(value)

    def kept(high, low, i):
        return high[i], low[i]

    for (j, m), value in couplings(couple, parent).items():
        keep(chigh, clow, at(m, j), value)
        keep(ihigh, ilow, at(m, j), -value)
    for gap in range(2, NSUP):
        for m in range(NSUP - gap):
            j = m + gap
            value = -(chigh[at(m, j)].astype(F32) + clow[at(m, j)].astype(F32))
            for q in range(m + 1, j):
                value = value - mul(kept(ihigh, ilow, at(m, q)), kept(chigh, clow, at(q, j)))
            keep(ihigh, ilow, at(m, j), value)
    for q in range(NSUP):
        out[at(q, q) * W : (at(q, q) + 1) * W, :] = diag_inv[q]
        keep(shigh, slow, at(q, q), diag_inv[q])
    split, rows = base_tables(order)

    def scale(t, carry):
        i = table[t, 0]
        value = mul(kept(shigh, slow, table[t, 1]), kept(ihigh, ilow, table[t, 2]))
        out[pl.ds(pl.multiple_of(i * W, W), W), :] = value
        keep(shigh, slow, i, value)
        return carry

    def gain(t, carry):
        where = pl.ds(pl.multiple_of(table[t, 0] * W, W), W)
        left, right = kept(ihigh, ilow, table[t, 1]), kept(shigh, slow, table[t, 2])
        out[where, :] = out[where, :] + mul(left, right, (0, 0))
        return carry

    lax.fori_loop(0, split, scale, 0)
    lax.fori_loop(split, len(rows), gain, 0)
    for i in TURNED:
        where = slice(i * W, (i + 1) * W)
        out[where, :] = out[where, :].T


def put(piece, top, bot, row_of):
    def step(r, carry):
        src = pl.multiple_of(r * RW, 16)
        dst = pl.multiple_of(row_of(r), 16)
        hi, lo = halves(piece[pl.ds(src, RW), :])
        top[pl.ds(dst, RW), :] = hi
        bot[pl.ds(dst, RW), :] = lo
        return carry

    lax.fori_loop(0, piece.shape[0] // RW, step, 0)


def near_kernel(local, near, twin, cross, out, ltop, lbot, rtop, rbot, top, bot):
    at = place()
    span = local.shape[1] // 4
    for i, k in enumerate((0, 1, 3, 2)):
        src = pl.multiple_of(((at["y"] - k) & 3) * span, 128)

        def step(t, carry, src=src, i=i):
            rows = pl.ds(pl.multiple_of(t * RW, 16), RW)
            hi, lo = halves(local[rows, pl.ds(src, span)])
            ltop[rows, i * span : (i + 1) * span] = hi
            lbot[rows, i * span : (i + 1) * span] = lo
            return carry

        lax.fori_loop(0, local.shape[0] // RW, step, 0)
    put(cross, rtop, rbot, lambda r: ((at["x"] - r) & 3) * RW)
    for par, piece in enumerate((near, twin)):
        core = at["c"] ^ par
        put(piece, top, bot, lambda r: (((at["zl"] - r) & 3) * 2 + core) * RW)
    out[...] = mul((ltop[:, :span], lbot[:, :span]), (top[...], bot[...]))


def early_kernel(start, ltop, lbot, left, right, ltwin, rtwin, out, top, bot):
    at = place()
    span = ltop.shape[1] // 4
    for i, piece in enumerate((left, right, ltwin, rtwin)):
        core = at["c"] ^ (i // 2)
        put(piece, top, bot, lambda r: ((i % 2) * 8 + ((at["zl"] - r) & 3) * 2 + core) * RW)
    cols = slice(span, 3 * span)
    out[...] = start[...] + mul((ltop[:, cols], lbot[:, cols]), (top[...], bot[...]))


def late_kernel(*refs):
    early, ltop, lbot = refs[:3]
    pieces, outs = refs[3:7], refs[7:11]
    high, low, give = refs[11:14]
    top, bot, result = refs[14:]
    at = place()
    span = ltop.shape[1] // 4
    for i, piece in enumerate(pieces):
        core = at["c"] ^ (i // 2)
        start = 2 * (i % 2)
        put(piece, top, bot, lambda r: (((at["zl"] - r - start) & 3) * 2 + core) * RW)
    cols = slice(3 * span, 4 * span)
    result[...] = early[...] + mul((ltop[:, cols], lbot[:, cols]), (top[...], bot[...]))
    wide = give.shape[1]
    high[...], low[...] = halves(result[:, pl.ds(pl.multiple_of(at["c"] * wide, wide), wide)])
    give[...] = result[:, pl.ds(pl.multiple_of((1 - at["c"]) * wide, wide), wide)]
    for k, out in enumerate(outs):
        xa = (at["x"] + k) & 3
        for r in range(2):
            out[r] = result[pl.ds(pl.multiple_of((r * 4 + xa) * RW, 16), RW), :]


def rows_kernel(ra, rb, distant, cross2, distant2, rtop, rbot):
    at = place()
    quad = ra.shape[0]
    here = pl.ds(pl.multiple_of(at["zh"] * quad, 16), quad)
    rtop[here, :] = ra[...]
    rbot[here, :] = rb[...]
    for base, side, piece in ((0, 1 - at["zh"], distant), (2, at["zh"], cross2), (2, 1 - at["zh"], distant2)):
        put(piece, rtop, rbot, lambda r: (base + side) * quad + ((at["x"] - r) & 3) * RW)


def window_kernel(high, low, got, rtop, rbot, base, *refs):
    outs, (top, bot, whole) = refs[:4], refs[4:]
    at = place()
    rows = high.shape[0]
    top[:rows, :] = high[...]
    bot[:rows, :] = low[...]
    top[rows:, :], bot[rows:, :] = halves(got[...])
    lead = (lax.axis_index("row") == 0) & (lax.axis_index("col") < 2)
    for i, (one, two) in enumerate(zip(*BLOCKS)):
        pick = lambda a, b: pl.ds(pl.multiple_of(jnp.where(at["c"] == 0, a, b) * W, W), W)
        left, right = pick(one[0], two[0]), pick(one[1], two[1] - 2)
        block = mul((rtop[:, left], rbot[:, left]), (top[:, right], bot[:, right]), (0, 0))
        plus = base[pl.ds(pl.multiple_of(at["c"] * (len(BLOCKS[0]) * W) + i * W, W), W), :]
        whole[i * W : (i + 1) * W, :] = block + jnp.where(lead, plus, 0.0)
    size = outs[0].shape[0]
    for k, out in enumerate(outs):
        out[...] = whole[pl.ds(pl.multiple_of(((at["y"] + k) & 3) * size, 8), size), :]


def pick_kernel(*refs):
    pieces, keep, give = refs[:4], refs[4], refs[5]
    zh = place()["zh"]
    for out, side in ((keep, zh), (give, 1 - zh)):
        total = pieces[0][side]
        for piece in pieces[1:]:
            total = total + piece[side]
        out[...] = total


def columns_kernel(keep, got, out):
    for j in range(NSUP):
        cols = slice(j * W, (j + 1) * W)
        out[j] = -(keep[:, cols] + got[:, cols])


def join_kernel(axis, *refs):
    pieces, out = refs[:-1], refs[-1]
    at = place()[axis]
    rows = pieces[0].shape[0]
    for k, piece in enumerate(pieces):
        dst = pl.multiple_of(((at - k) & (SIZES[axis] - 1)) * rows, 8)
        out[pl.ds(dst, rows), :] = piece[...]


def add_split_kernel(axis, count, *refs):
    values, outs = refs[:count], refs[count:]
    at = place()[axis]
    rows = outs[0].shape[0]
    for k, out in enumerate(outs):
        src = pl.ds(pl.multiple_of(((at + k) & (SIZES[axis] - 1)) * rows, 8), rows)
        total = values[0][src, :]
        for value in values[1:]:
            total = total + value[src, :]
        out[...] = total


def final_kernel(*refs):
    pieces, pair_out, diag_out, whole = refs[:8], refs[8], refs[9], refs[10]
    at = place()
    rows = pieces[0].shape[0]
    for par in range(2):
        core = at["c"] ^ par
        for k in range(4):
            dst = pl.multiple_of(((at["y"] - k) & 3) * rows, 8)
            whole[pl.ds(dst, rows), :] = pieces[par * 4 + k][...]

        @pl.when(core == 0)
        def _():
            for i in TURNED:
                whole[i * W : (i + 1) * W, :] = whole[i * W : (i + 1) * W, :].T

        for i in range(3):
            pair_out[core * 3 + i] = whole[i * W : (i + 1) * W, :]
        for i in range(2):
            diag_out[core * 2 + i] = whole[(3 + i) * W : (4 + i) * W, :]


def kernel(body, args, out_shapes, scratch=(), smem=0, flops=0):
    single = not isinstance(out_shapes, list)
    return pl.pallas_call(
        body,
        out_shape=jax.ShapeDtypeStruct(out_shapes, F32)
        if single
        else [jax.ShapeDtypeStruct(s, F32) if isinstance(s[-1], int) else jax.ShapeDtypeStruct(*s) for s in out_shapes],
        in_specs=[SMEM] * smem + [VMEM] * (len(args) - smem),
        out_specs=VMEM if single else [VMEM] * len(out_shapes),
        scratch_shapes=[pltpu.VMEM(s, t) for s, t in scratch],
        compiler_params=pltpu.CompilerParams(vmem_limit_bytes=56 << 20),
        cost_estimate=pl.CostEstimate(
            flops=flops, transcendentals=0, bytes_accessed=sum(4 * a.size for a in args)
        ),
    )(*args)


def split_sum(values, axis):
    rows, width = values[0].shape
    n = SIZES[axis]
    return kernel(
        functools.partial(add_split_kernel, axis, len(values)),
        list(values),
        [(rows // n, width)] * n,
    )


def scattered(pieces, axis):
    return [pieces[0]] + [moved(pieces[k], axis, k) for k in range(1, len(pieces))]


def gathered(value, axis):
    return [value] + [moved(value, axis, k) for k in range(1, SIZES[axis])]


def total_of(values):
    total = values[0]
    for value in values[1:]:
        total = total + value
    return total


def shards(inv_anc, factor_cols, couple, diag_inv, pattern, parent):
    local = inv_anc.reshape(-1, inv_anc.shape[3])
    height = local.shape[0]

    own = kernel(
        pre_kernel, [parent, pattern, factor_cols, couple], (RW, NSUP * W), smem=2, flops=1 << 20
    )
    width = NSUP * W
    tall = len(ALL_BLOCKS) * W
    span = local.shape[1] // 4

    near = gathered(own, "zl")
    cross = gathered(own, "x")
    _, couple_later = tie(own, couple)
    table = jnp.array(base_tables(ALL_BLOCKS)[1], jnp.int32)
    base = kernel(
        functools.partial(base_kernel, ALL_BLOCKS),
        [parent, table, couple_later, diag_inv],
        (tall, W),
        [((len(ALL_BLOCKS), W, W), BF16)] * 6,
        smem=2,
        flops=1 << 31,
    )
    near = jnp.concatenate(near, axis=0)
    near, base, *cross = tie(near, base, *cross)
    cross = jnp.concatenate(cross, axis=0)

    left, right = moved(near, "y", 1), moved(near, "y", 3)
    distant = moved(cross, "zh", 1)
    cross2 = moved(cross, "c", 1)
    start, ltop, lbot, ra, rb = kernel(
        near_kernel,
        [local, near, moved(near, "c", 1), cross],
        [(height, width)] + [((height, 4 * span), BF16)] * 2 + [(cross.shape, BF16)] * 2,
        [((span, width), BF16)] * 2,
        flops=1 << 31,
    )
    left, right, start = tie(left, right, start)
    half = near.shape[0] // 2
    far_a, far_b = moved(left[:half], "y", 1), moved(right[half:], "y", 3)
    early = kernel(
        early_kernel,
        [start, ltop, lbot, left, right, moved(left, "c", 1), moved(right, "c", 1)],
        (height, width),
        [((2 * span, width), BF16)] * 2,
        flops=1 << 31,
    )
    far_a, far_b, early = tie(far_a, far_b, early)
    *parts, high, low, give = kernel(
        late_kernel,
        [early, ltop, lbot, far_a, far_b, moved(far_a, "c", 1), moved(far_b, "c", 1)],
        [(2, RW, width)] * 4 + [((height, width // 2), BF16)] * 2 + [(height, width // 2)],
        [((span, width), BF16)] * 2 + [((height, width), F32)],
        flops=1 << 31,
    )

    got = moved(give, "c", 1)
    cols = scattered(parts, "x")
    rtop, rbot = kernel(
        rows_kernel,
        [ra, rb, distant, cross2, moved(distant, "c", 1)],
        [((2 * height, width), BF16)] * 2,
        flops=1 << 28,
    )
    cut = kernel(
        window_kernel,
        [high, low, got, rtop, rbot, base],
        [(tall // 8, W)] * 4,
        [((2 * height, width // 2), BF16)] * 2 + [((tall // 2, W), F32)],
        flops=1 << 31,
    )
    across = scattered(cut, "y")
    keep, give = kernel(pick_kernel, cols, [(RW, width)] * 2)
    summed = moved(give, "zh", 1)
    cut = split_sum(across, "x")
    total = total_of(scattered(cut, "x"))
    total = total + sent(total, "zl", lambda a: a ^ 1)
    total = total + sent(total, "zl", lambda a: a ^ 2)
    total = total + moved(total, "zh", 1)
    lines = gathered(total, "x")
    total = kernel(functools.partial(join_kernel, "x"), lines, (4 * total.shape[0], W))
    lanes = gathered(total, "y")
    twins = [moved(v, "c", 1) for v in lanes]
    pair_blocks, diagonal = kernel(
        final_kernel,
        lanes + twins,
        [(len(PAIRS), W, W), (NSUP, W, W)],
        [((tall // 2, W), F32)],
    )
    keep, pair_blocks, diagonal = tie(keep, pair_blocks, diagonal)
    columns = kernel(columns_kernel, [keep, summed], (NSUP, RW, W))
    return (columns, pair_blocks, diagonal)


def solution(mesh):
    in_specs = (P(None, "col", None, "row"), P(None, BOTH, None), P(), P(), P(), P())
    out_specs = (P(None, BOTH, None), P(), P())

    return jax.shard_map(shards, mesh=mesh, in_specs=in_specs, out_specs=out_specs, check_vma=False)
```

```python
import functools

import jax
import jax.numpy as jnp
from jax import lax
from jax.experimental import pallas as pl
from jax.experimental.pallas import tpu as pltpu
from jax.sharding import PartitionSpec as P


W = 256
NSUP = 4
RW = 48
HALF = W // 2
SIZES = {"zh": 2, "x": 4, "y": 4, "zl": 4, "c": 2}
BOTH = ("row", "col")
F32, BF16 = jnp.float32, jnp.bfloat16
PAIRS = [(m, j) for j in range(NSUP) for m in range(j)]
ALL_BLOCKS = PAIRS + [(j, j) for j in range(NSUP)]
VMEM = pl.BlockSpec(memory_space=pltpu.VMEM)
SMEM = pl.BlockSpec(memory_space=pltpu.SMEM)


def place():
    row, col = lax.axis_index("row"), lax.axis_index("col")
    return {"zh": row >> 2, "x": row & 3, "y": col >> 3, "zl": (col >> 1) & 3, "c": col & 1}


def moved(value, axis, step):
    return sent(value, axis, lambda a: (a + step) % SIZES[axis])


def sent(value, axis, rule):
    names = list(SIZES)
    perm = []
    for device in range(256):
        rest, at = device, {}
        for name in reversed(names):
            at[name] = rest % SIZES[name]
            rest //= SIZES[name]
        at[axis] = rule(at[axis])
        target = 0
        for name in names:
            target = target * SIZES[name] + at[name]
        perm.append((device, target))
    return lax.ppermute(value, BOTH, perm)


def tie(*values):
    return lax.optimization_barrier(values)


def halves(value):
    top = value.astype(BF16)
    return top, (value - top.astype(F32)).astype(BF16)


def mul(left, right, over=(1, 0)):
    dims = (((over[0],), (over[1],)), ((), ()))
    dot = lambda u, v: lax.dot_general(u, v, dims, preferred_element_type=F32)
    return dot(left[0], right[0]) + (dot(left[1], right[0]) + dot(left[0], right[1]))


def couplings(couple, parent):
    linked = {}
    blocks = {}
    for j in range(NSUP):
        for m in range(j):
            now = parent[j] == m
            for p in range(m + 1, j):
                now = now | ((parent[j] == p) & linked[p, m])
            linked[j, m] = now
            blocks[j, m] = couple[j * (j - 1) // 2 + m] * jnp.where(now, 1.0, 0.0).astype(F32)
    return blocks


def pre_kernel(parent, pattern, factor, couple, out):
    first = (lax.axis_index("row") * 32 + lax.axis_index("col")) * RW
    block = first >> 8
    after = jnp.minimum(block + 1, pattern.shape[1] - 1)
    edge = (block + 1) * W - first
    low = lax.broadcasted_iota(jnp.int32, (RW, W), 0) < edge
    blocks = couplings(couple, parent)
    values = []
    for j in range(NSUP):
        here, there = pattern[j, block].astype(F32), pattern[j, after].astype(F32)
        values.append(factor[j] * jnp.where(low, here, there))
    for m in range(NSUP):
        out[:, m * W : (m + 1) * W] = values[m]
        left = halves(values[m])
        for j in range(m + 1, NSUP):
            values[j] = values[j] - mul(left, halves(blocks[j, m]))


def base_kernel(order, parent, couple, diag_inv, out, *held):
    chigh, clow, ihigh, ilow, shigh, slow = held
    at = lambda q, j: order.index((q, j))

    def keep(high, low, i, value):
        high[i], low[i] = halves(value)

    def kept(high, low, i):
        return high[i], low[i]

    for (j, m), value in couplings(couple, parent).items():
        keep(chigh, clow, at(m, j), value)
        keep(ihigh, ilow, at(m, j), -value)
    for gap in range(2, NSUP):
        for m in range(NSUP - gap):
            j = m + gap
            value = -(chigh[at(m, j)].astype(F32) + clow[at(m, j)].astype(F32))
            for q in range(m + 1, j):
                value = value - mul(kept(ihigh, ilow, at(m, q)), kept(chigh, clow, at(q, j)))
            keep(ihigh, ilow, at(m, j), value)
    for q in range(NSUP):
        out[at(q, q) * W : (at(q, q) + 1) * W, :] = diag_inv[q]
        keep(shigh, slow, at(q, q), diag_inv[q])
        for j in range(q + 1, NSUP):
            i = at(q, j)
            value = mul(kept(shigh, slow, at(q, q)), kept(ihigh, ilow, i))
            out[i * W : (i + 1) * W, :] = value
            keep(shigh, slow, i, value)
    for i, (m, j) in enumerate(order):
        rows = slice(i * W, (i + 1) * W)
        for q in range(m):
            out[rows, :] = out[rows, :] + mul(kept(ihigh, ilow, at(q, m)), kept(shigh, slow, at(q, j)), (0, 0))


def put(piece, top, bot, row_of, weight=None):
    def step(r, carry):
        src = pl.multiple_of(r * RW, 16)
        dst = pl.multiple_of(row_of(r), 16)
        value = piece[pl.ds(src, RW), :]
        hi, lo = halves(value if weight is None else value * weight(r))
        top[pl.ds(dst, RW), :] = hi
        bot[pl.ds(dst, RW), :] = lo
        return carry

    lax.fori_loop(0, piece.shape[0] // RW, step, 0)


def near_kernel(local, near, twin, cross, out, ltop, lbot, rtop, rbot, top, bot):
    at = place()
    span = local.shape[1] // 4
    for i, k in enumerate((0, 1, 3, 2)):
        src = pl.multiple_of(((at["y"] - k) & 3) * span, 128)

        def step(t, carry, src=src, i=i):
            rows = pl.ds(pl.multiple_of(t * RW, 16), RW)
            hi, lo = halves(local[rows, pl.ds(src, span)])
            ltop[rows, i * span : (i + 1) * span] = hi
            lbot[rows, i * span : (i + 1) * span] = lo
            return carry

        lax.fori_loop(0, local.shape[0] // RW, step, 0)
    put(cross, rtop, rbot, lambda r: r * RW, lambda r: jnp.where(r == 1, 1.0, 0.5).astype(F32))
    for par, piece in enumerate((near, twin)):
        core = at["c"] ^ par
        put(piece, top, bot, lambda r: (((at["zl"] - r) & 3) * 2 + core) * RW)
    out[...] = mul((ltop[:, :span], lbot[:, :span]), (top[...], bot[...]))


def early_kernel(start, ltop, lbot, left, right, ltwin, rtwin, out, top, bot):
    at = place()
    span = ltop.shape[1] // 4
    for i, piece in enumerate((left, right, ltwin, rtwin)):
        core = at["c"] ^ (i // 2)
        put(piece, top, bot, lambda r: ((i % 2) * 8 + ((at["zl"] - r) & 3) * 2 + core) * RW)
    cols = slice(span, 3 * span)
    out[...] = start[...] + mul((ltop[:, cols], lbot[:, cols]), (top[...], bot[...]))


def main_kernel(order, *refs):
    early, base, ltop, lbot, ra, rb, distant = refs[:7]
    pieces, outs = refs[7:11], refs[11:15]
    kept, given = refs[15], refs[16]
    top, bot, rtop, rbot, result, ptop, pbot = refs[17:]
    at = place()
    span = ltop.shape[1] // 4
    quad = ra.shape[0]
    for i, piece in enumerate(pieces):
        core = at["c"] ^ (i // 2)
        start = 2 * (i % 2)
        put(piece, top, bot, lambda r: (((at["zl"] - r - start) & 3) * 2 + core) * RW)
    rtop[:quad, :] = ra[...]
    rbot[:quad, :] = rb[...]
    put(distant, rtop, rbot, lambda r: quad + r * RW)
    cols = slice(3 * span, 4 * span)
    value = early[...] + mul((ltop[:, cols], lbot[:, cols]), (top[...], bot[...]))
    result[...] = value
    taken = [at["zh"] * 4 + ((at["x"] + k) & 3) for k in range(3)]
    taken += [(1 - at["zh"]) * 4 + ((at["x"] + k + at["zh"]) & 3) for k in range(2)]
    for i, block in enumerate(taken):
        hi, lo = halves(result[pl.ds(pl.multiple_of(block * RW, 16), RW), :])
        ptop[i * RW : (i + 1) * RW, :] = hi
        pbot[i * RW : (i + 1) * RW, :] = lo
    for k, out in enumerate(outs):
        xa = (at["x"] + k) & 3
        for r in range(2):
            out[r] = result[pl.ds(pl.multiple_of((r * 4 + xa) * RW, 16), RW), :]
    lead = (lax.axis_index("row") == 0) & (lax.axis_index("col") == 0)
    even = at["c"] == 0
    for i, (m, j) in enumerate(order):
        one, two = slice(m * W, (m + 1) * W), slice(j * W, (j + 1) * W)
        block = mul((rtop[:, one], rbot[:, one]), (ptop[:, two], pbot[:, two]), (0, 0))
        block = block + mul((ptop[:, one], pbot[:, one]), (rtop[:, two], rbot[:, two]), (0, 0))
        rows = slice(i * W, (i + 1) * W)
        block = block + jnp.where(lead, base[rows, :], 0.0)
        first, second = block[:, :HALF], block[:, HALF:]
        kept[rows, :] = jnp.where(even, first, second)
        given[rows, :] = jnp.where(even, second, first)


def pick_kernel(*refs):
    pieces, keep, give = refs[:4], refs[4], refs[5]
    zh = place()["zh"]
    for out, side in ((keep, zh), (give, 1 - zh)):
        total = pieces[0][side]
        for piece in pieces[1:]:
            total = total + piece[side]
        out[...] = total


def columns_kernel(keep, got, out):
    for j in range(NSUP):
        cols = slice(j * W, (j + 1) * W)
        out[j] = -(keep[:, cols] + got[:, cols])


def join_kernel(axis, *refs):
    pieces, out = refs[:-1], refs[-1]
    at = place()[axis]
    rows = pieces[0].shape[0]
    for k, piece in enumerate(pieces):
        dst = pl.multiple_of(((at - k) & (SIZES[axis] - 1)) * rows, 8)
        out[pl.ds(dst, rows), :] = piece[...]


def add_split_kernel(axis, count, *refs):
    values, outs = refs[:count], refs[count:]
    at = place()[axis]
    rows = outs[0].shape[0]
    for k, out in enumerate(outs):
        src = pl.ds(pl.multiple_of(((at + k) & (SIZES[axis] - 1)) * rows, 8), rows)
        total = values[0][src, :]
        for value in values[1:]:
            total = total + value[src, :]
        out[...] = total


def final_kernel(orders, *refs):
    count = 8 * len(orders)
    pieces, pair_out, diag_out, wholes = refs[:count], refs[count], refs[count + 1], refs[count + 2 :]
    at = place()
    for i, order in enumerate(orders):
        whole = wholes[i]
        for par in range(2):
            for k in range(4):
                piece = pieces[i * 8 + par * 4 + k]
                rows = piece.shape[0]
                dst = pl.multiple_of(((at["y"] - k) & 3) * rows, 8)
                lane = pl.multiple_of((at["c"] ^ par) * HALF, HALF)
                whole[pl.ds(dst, rows), pl.ds(lane, HALF)] = piece[...]
        for b, (m, j) in enumerate(order):
            rows = slice(b * W, (b + 1) * W)
            if m == j:
                diag_out[j] = whole[rows, :]
            else:
                pair_out[PAIRS.index((m, j))] = whole[rows, :]


def kernel(body, args, out_shapes, scratch=(), smem=0, flops=0):
    single = not isinstance(out_shapes, list)
    return pl.pallas_call(
        body,
        out_shape=jax.ShapeDtypeStruct(out_shapes, F32)
        if single
        else [jax.ShapeDtypeStruct(s, F32) if isinstance(s[-1], int) else jax.ShapeDtypeStruct(*s) for s in out_shapes],
        in_specs=[SMEM] * smem + [VMEM] * (len(args) - smem),
        out_specs=VMEM if single else [VMEM] * len(out_shapes),
        scratch_shapes=[pltpu.VMEM(s, t) for s, t in scratch],
        compiler_params=pltpu.CompilerParams(vmem_limit_bytes=56 << 20),
        cost_estimate=pl.CostEstimate(
            flops=flops, transcendentals=0, bytes_accessed=sum(4 * a.size for a in args)
        ),
    )(*args)


def split_sum(values, axis):
    rows, width = values[0].shape
    n = SIZES[axis]
    return kernel(
        functools.partial(add_split_kernel, axis, len(values)),
        list(values),
        [(rows // n, width)] * n,
    )


def scattered(pieces, axis):
    return [pieces[0]] + [moved(pieces[k], axis, k) for k in range(1, len(pieces))]


def gathered(value, axis):
    return [value] + [moved(value, axis, k) for k in range(1, SIZES[axis])]


def total_of(values):
    total = values[0]
    for value in values[1:]:
        total = total + value
    return total


def shards(inv_anc, factor_cols, couple, diag_inv, pattern, parent):
    at = place()
    local = inv_anc.reshape(-1, inv_anc.shape[3])
    height = local.shape[0]

    own = kernel(
        pre_kernel, [parent, pattern, factor_cols, couple], (RW, NSUP * W), smem=2, flops=1 << 20
    )
    width = NSUP * W
    tall = len(ALL_BLOCKS) * W
    span = local.shape[1] // 4

    near = gathered(own, "zl")
    cross = [own, moved(own, "x", 3), moved(own, "x", 2)]
    _, couple_later = tie(own, couple)
    base = kernel(
        functools.partial(base_kernel, ALL_BLOCKS),
        [parent, couple_later, diag_inv],
        (tall, W),
        [((len(ALL_BLOCKS), W, W), BF16)] * 6,
        smem=1,
        flops=1 << 31,
    )
    near = jnp.concatenate(near, axis=0)
    near, base = tie(near, base)
    cross = jnp.concatenate(cross, axis=0)

    left, right = moved(near, "y", 1), moved(near, "y", 3)
    distant = moved(lax.dynamic_slice_in_dim(cross, (1 - at["zh"]) * RW, 2 * RW, 0), "zh", 1)
    start, ltop, lbot, ra, rb = kernel(
        near_kernel,
        [local, near, moved(near, "c", 1), cross],
        [(height, width)] + [((height, 4 * span), BF16)] * 2 + [(cross.shape, BF16)] * 2,
        [((span, width), BF16)] * 2,
        flops=1 << 31,
    )
    left, right, start = tie(left, right, start)
    half = near.shape[0] // 2
    far_a, far_b = moved(left[:half], "y", 1), moved(right[half:], "y", 3)
    early = kernel(
        early_kernel,
        [start, ltop, lbot, left, right, moved(left, "c", 1), moved(right, "c", 1)],
        (height, width),
        [((2 * span, width), BF16)] * 2,
        flops=1 << 31,
    )
    far_a, far_b, early = tie(far_a, far_b, early)
    *parts, kept, given = kernel(
        functools.partial(main_kernel, ALL_BLOCKS),
        [early, base, ltop, lbot, ra, rb, distant]
        + [far_a, far_b, moved(far_a, "c", 1), moved(far_b, "c", 1)],
        [(2, RW, width)] * 4 + [(tall, HALF)] * 2,
        [((span, width), BF16)] * 2
        + [((5 * RW, width), BF16)] * 2
        + [((height, width), F32)]
        + [((5 * RW, width), BF16)] * 2,
        flops=1 << 32,
    )

    got = moved(given, "c", 1)
    cut = split_sum([kept, got], "y")
    cols = scattered(parts, "x")
    across = scattered(cut, "y")
    keep, give = kernel(pick_kernel, cols, [(RW, width)] * 2)
    summed = moved(give, "zh", 1)
    cut = split_sum(across, "x")
    total = total_of(scattered(cut, "x"))
    total = total + sent(total, "zl", lambda a: a ^ 1)
    total = total + sent(total, "zl", lambda a: a ^ 2)
    total = total + moved(total, "zh", 1)
    lines = gathered(total, "x")
    total = kernel(functools.partial(join_kernel, "x"), lines, (4 * total.shape[0], HALF))
    lanes = gathered(total, "y")
    twins = [moved(v, "c", 1) for v in lanes]
    pair_blocks, diagonal = kernel(
        functools.partial(final_kernel, [ALL_BLOCKS]),
        lanes + twins,
        [(len(PAIRS), W, W), (NSUP, W, W)],
        [((tall, W), F32)],
    )
    keep, pair_blocks, diagonal = tie(keep, pair_blocks, diagonal)
    columns = kernel(columns_kernel, [keep, summed], (NSUP, RW, W))
    return (columns, pair_blocks, diagonal)


def solution(mesh):
    in_specs = (P(None, "col", None, "row"), P(None, BOTH, None), P(), P(), P(), P())
    out_specs = (P(None, BOTH, None), P(), P())

    return jax.shard_map(shards, mesh=mesh, in_specs=in_specs, out_specs=out_specs, check_vma=False)
```

```python
import functools

import jax
import jax.numpy as jnp
from jax import lax
from jax.experimental import pallas as pl
from jax.experimental.pallas import tpu as pltpu
from jax.sharding import PartitionSpec as P


W = 256
NSUP = 4
RW = 48
HALF = W // 2
SIZES = {"zh": 2, "x": 4, "y": 4, "zl": 4, "c": 2}
BOTH = ("row", "col")
F32, BF16 = jnp.float32, jnp.bfloat16
PAIRS = [(m, j) for j in range(NSUP) for m in range(j)]
ALL_BLOCKS = PAIRS + [(j, j) for j in range(NSUP)]
VMEM = pl.BlockSpec(memory_space=pltpu.VMEM)
SMEM = pl.BlockSpec(memory_space=pltpu.SMEM)


def place():
    row, col = lax.axis_index("row"), lax.axis_index("col")
    return {"zh": row >> 2, "x": row & 3, "y": col >> 3, "zl": (col >> 1) & 3, "c": col & 1}


def moved(value, axis, step):
    return sent(value, axis, lambda a: (a + step) % SIZES[axis])


def sent(value, axis, rule):
    names = list(SIZES)
    perm = []
    for device in range(256):
        rest, at = device, {}
        for name in reversed(names):
            at[name] = rest % SIZES[name]
            rest //= SIZES[name]
        at[axis] = rule(at[axis])
        target = 0
        for name in names:
            target = target * SIZES[name] + at[name]
        perm.append((device, target))
    return lax.ppermute(value, BOTH, perm)


def tie(*values):
    return lax.optimization_barrier(values)


def halves(value):
    top = value.astype(BF16)
    return top, (value - top.astype(F32)).astype(BF16)


def mul(left, right, over=(1, 0)):
    dims = (((over[0],), (over[1],)), ((), ()))
    dot = lambda u, v: lax.dot_general(u, v, dims, preferred_element_type=F32)
    return dot(left[0], right[0]) + (dot(left[1], right[0]) + dot(left[0], right[1]))


def couplings(couple, parent):
    linked = {}
    blocks = {}
    for j in range(NSUP):
        for m in range(j):
            now = parent[j] == m
            for p in range(m + 1, j):
                now = now | ((parent[j] == p) & linked[p, m])
            linked[j, m] = now
            blocks[j, m] = couple[j * (j - 1) // 2 + m] * jnp.where(now, 1.0, 0.0).astype(F32)
    return blocks


def pre_kernel(parent, pattern, factor, couple, out):
    first = (lax.axis_index("row") * 32 + lax.axis_index("col")) * RW
    block = first >> 8
    after = jnp.minimum(block + 1, pattern.shape[1] - 1)
    edge = (block + 1) * W - first
    low = lax.broadcasted_iota(jnp.int32, (RW, W), 0) < edge
    blocks = couplings(couple, parent)
    values = []
    for j in range(NSUP):
        here, there = pattern[j, block].astype(F32), pattern[j, after].astype(F32)
        values.append(factor[j] * jnp.where(low, here, there))
    for m in range(NSUP):
        out[:, m * W : (m + 1) * W] = values[m]
        left = halves(values[m])
        for j in range(m + 1, NSUP):
            values[j] = values[j] - mul(left, halves(blocks[j, m]))


def base_table(order):
    at = lambda q, j: order.index((q, j))
    return [(at(m, j), at(q, m), at(q, j)) for j in range(NSUP) for m in range(j + 1) for q in range(m)]


def base_kernel(order, parent, table, couple, diag_inv, out, *held):
    chigh, clow, ihigh, ilow, shigh, slow = held
    at = lambda q, j: order.index((q, j))

    def keep(high, low, i, value):
        high[i], low[i] = halves(value)

    def kept(high, low, i):
        return high[i], low[i]

    for (j, m), value in couplings(couple, parent).items():
        keep(chigh, clow, at(m, j), value)
        keep(ihigh, ilow, at(m, j), -value)
    for gap in range(2, NSUP):
        for m in range(NSUP - gap):
            j = m + gap
            value = -(chigh[at(m, j)].astype(F32) + clow[at(m, j)].astype(F32))
            for q in range(m + 1, j):
                value = value - mul(kept(ihigh, ilow, at(m, q)), kept(chigh, clow, at(q, j)))
            keep(ihigh, ilow, at(m, j), value)
    for q in range(NSUP):
        out[at(q, q) * W : (at(q, q) + 1) * W, :] = diag_inv[q]
        keep(shigh, slow, at(q, q), diag_inv[q])
        for j in range(q + 1, NSUP):
            i = at(q, j)
            value = mul(kept(shigh, slow, at(q, q)), kept(ihigh, ilow, i))
            out[i * W : (i + 1) * W, :] = value
            keep(shigh, slow, i, value)

    def gain(t, carry):
        where = pl.ds(pl.multiple_of(table[t, 0] * W, W), W)
        left, right = kept(ihigh, ilow, table[t, 1]), kept(shigh, slow, table[t, 2])
        out[where, :] = out[where, :] + mul(left, right, (0, 0))
        return carry

    lax.fori_loop(0, len(base_table(order)), gain, 0)


def put(piece, top, bot, row_of, weight=None):
    def step(r, carry):
        src = pl.multiple_of(r * RW, 16)
        dst = pl.multiple_of(row_of(r), 16)
        value = piece[pl.ds(src, RW), :]
        hi, lo = halves(value if weight is None else value * weight(r))
        top[pl.ds(dst, RW), :] = hi
        bot[pl.ds(dst, RW), :] = lo
        return carry

    lax.fori_loop(0, piece.shape[0] // RW, step, 0)


def near_kernel(local, own, rest, twin, cross, out, ltop, lbot, rtop, rbot, top, bot):
    at = place()
    span = local.shape[1] // 4
    for i, k in enumerate((0, 1, 3, 2)):
        src = pl.multiple_of(((at["y"] - k) & 3) * span, 128)

        def step(t, carry, src=src, i=i):
            rows = pl.ds(pl.multiple_of(t * RW, 16), RW)
            hi, lo = halves(local[rows, pl.ds(src, span)])
            ltop[rows, i * span : (i + 1) * span] = hi
            lbot[rows, i * span : (i + 1) * span] = lo
            return carry

        lax.fori_loop(0, local.shape[0] // RW, step, 0)
    put(cross, rtop, rbot, lambda r: r * RW, lambda r: jnp.where(r == 1, 1.0, 0.5).astype(F32))
    for piece, par, skip in ((own, 0, 0), (rest, 0, 1), (twin, 1, 0)):
        core = at["c"] ^ par
        put(piece, top, bot, lambda r: (((at["zl"] - r - skip) & 3) * 2 + core) * RW)
    out[...] = mul((ltop[:, :span], lbot[:, :span]), (top[...], bot[...]))


def early_kernel(start, ltop, lbot, *refs):
    pieces, (out, top, bot) = refs[:6], refs[6:]
    at = place()
    span = ltop.shape[1] // 4
    for i, piece in enumerate(pieces):
        core = at["c"] ^ (i // 3)
        if i % 3 == 0:
            put(piece, top, bot, lambda r: (r * 8 + at["zl"] * 2 + core) * RW)
        else:
            side = i % 3 - 1
            put(piece, top, bot, lambda r: (side * 8 + ((at["zl"] - r - 1) & 3) * 2 + core) * RW)
    cols = slice(span, 3 * span)
    out[...] = start[...] + mul((ltop[:, cols], lbot[:, cols]), (top[...], bot[...]))


def main_kernel(order, *refs):
    early, base, ltop, lbot, ra, rb, distant = refs[:7]
    pieces, outs = refs[7:11], refs[11:15]
    kept, given = refs[15], refs[16]
    top, bot, rtop, rbot, result, ptop, pbot = refs[17:]
    at = place()
    span = ltop.shape[1] // 4
    quad = ra.shape[0]
    for i, piece in enumerate(pieces):
        core = at["c"] ^ (i // 2)
        start = 2 * (i % 2)
        put(piece, top, bot, lambda r: (((at["zl"] - r - start) & 3) * 2 + core) * RW)
    rtop[:quad, :] = ra[...]
    rbot[:quad, :] = rb[...]
    put(distant, rtop, rbot, lambda r: quad + r * RW)
    cols = slice(3 * span, 4 * span)
    value = early[...] + mul((ltop[:, cols], lbot[:, cols]), (top[...], bot[...]))
    result[...] = value
    taken = [at["zh"] * 4 + ((at["x"] + k) & 3) for k in range(3)]
    taken += [(1 - at["zh"]) * 4 + ((at["x"] + k + at["zh"]) & 3) for k in range(2)]
    for i, block in enumerate(taken):
        hi, lo = halves(result[pl.ds(pl.multiple_of(block * RW, 16), RW), :])
        ptop[i * RW : (i + 1) * RW, :] = hi
        pbot[i * RW : (i + 1) * RW, :] = lo
    for k, out in enumerate(outs):
        xa = (at["x"] + k) & 3
        for r in range(2):
            out[r] = result[pl.ds(pl.multiple_of((r * 4 + xa) * RW, 16), RW), :]
    lead = (lax.axis_index("row") == 0) & (lax.axis_index("col") == 0)
    even = at["c"] == 0
    for i, (m, j) in enumerate(order):
        one, two = slice(m * W, (m + 1) * W), slice(j * W, (j + 1) * W)
        block = mul((rtop[:, one], rbot[:, one]), (ptop[:, two], pbot[:, two]), (0, 0))
        if m == j:
            block = block + block.T
        else:
            block = block + mul((ptop[:, one], pbot[:, one]), (rtop[:, two], rbot[:, two]), (0, 0))
        rows = slice(i * W, (i + 1) * W)
        block = block + jnp.where(lead, base[rows, :], 0.0)
        first, second = block[:, :HALF], block[:, HALF:]
        kept[rows, :] = jnp.where(even, first, second)
        given[rows, :] = jnp.where(even, second, first)


def pick_kernel(*refs):
    pieces, keep, give = refs[:4], refs[4], refs[5]
    zh = place()["zh"]
    for out, side in ((keep, zh), (give, 1 - zh)):
        total = pieces[0][side]
        for piece in pieces[1:]:
            total = total + piece[side]
        out[...] = total


def final_kernel(order, *refs):
    pieces, (keep, got) = refs[:8], refs[8:10]
    columns, pair_out, diag_out, whole = refs[10:]
    at = place()
    rows = pieces[0].shape[0]
    small = rows // 4
    for i, piece in enumerate(pieces):
        par, k = divmod(i, 4)
        lane = pl.multiple_of((at["c"] ^ par) * HALF, HALF)
        for r in range(4):
            dst = pl.multiple_of(((at["y"] - k) & 3) * rows + ((at["x"] - r) & 3) * small, 8)
            whole[pl.ds(dst, small), pl.ds(lane, HALF)] = piece[r * small : (r + 1) * small, :]
    for b, (m, j) in enumerate(order):
        block = whole[b * W : (b + 1) * W, :]
        if m == j:
            diag_out[j] = block
        else:
            pair_out[PAIRS.index((m, j))] = block
    for j in range(NSUP):
        cols = slice(j * W, (j + 1) * W)
        columns[j] = -(keep[:, cols] + got[:, cols])


def kernel(body, args, out_shapes, scratch=(), smem=0, flops=0):
    single = not isinstance(out_shapes, list)
    return pl.pallas_call(
        body,
        out_shape=jax.ShapeDtypeStruct(out_shapes, F32)
        if single
        else [jax.ShapeDtypeStruct(s, F32) if isinstance(s[-1], int) else jax.ShapeDtypeStruct(*s) for s in out_shapes],
        in_specs=[SMEM] * smem + [VMEM] * (len(args) - smem),
        out_specs=VMEM if single else [VMEM] * len(out_shapes),
        scratch_shapes=[pltpu.VMEM(s, t) for s, t in scratch],
        compiler_params=pltpu.CompilerParams(vmem_limit_bytes=56 << 20),
        cost_estimate=pl.CostEstimate(
            flops=flops, transcendentals=0, bytes_accessed=sum(4 * a.size for a in args)
        ),
    )(*args)


def split_sum(values, at, axis):
    n = SIZES[axis]
    rows = values[0].shape[0] // n
    part = lambda v, k: lax.dynamic_slice_in_dim(v, ((at[axis] + k) & (n - 1)) * rows, rows, 0)
    return [total_of([part(v, k) for v in values]) for k in range(n)]


def scattered(pieces, axis):
    return [pieces[0]] + [moved(pieces[k], axis, k) for k in range(1, len(pieces))]


def gathered(value, axis):
    return [value] + [moved(value, axis, k) for k in range(1, SIZES[axis])]


def total_of(values):
    total = values[0]
    for value in values[1:]:
        total = total + value
    return total


def shards(inv_anc, factor_cols, couple, diag_inv, pattern, parent):
    at = place()
    local = inv_anc.reshape(-1, inv_anc.shape[3])
    height = local.shape[0]

    own = kernel(
        pre_kernel, [parent, pattern, factor_cols, couple], (RW, NSUP * W), smem=2, flops=1 << 20
    )
    width = NSUP * W
    tall = len(ALL_BLOCKS) * W
    span = local.shape[1] // 4

    near = gathered(own, "zl")
    firsts = [moved(own, "y", 1), moved(own, "y", 3)]
    cross = [own, moved(own, "x", 3), moved(own, "x", 2)]
    _, couple_later = tie(own, couple)
    base = kernel(
        functools.partial(base_kernel, ALL_BLOCKS),
        [parent, jnp.array(base_table(ALL_BLOCKS), jnp.int32), couple_later, diag_inv],
        (tall, W),
        [((len(ALL_BLOCKS), W, W), BF16)] * 6,
        smem=2,
        flops=1 << 31,
    )
    rest = jnp.concatenate(near[1:], axis=0)
    rest, base = tie(rest, base)
    both = jnp.concatenate(firsts, axis=0)
    cross, both = tie(jnp.concatenate(cross, axis=0), both)

    left, right = moved(rest, "y", 1), moved(rest, "y", 3)
    distant = moved(lax.dynamic_slice_in_dim(cross, (1 - at["zh"]) * RW, 2 * RW, 0), "zh", 1)
    twin = moved(jnp.concatenate([own, rest], axis=0), "c", 1)
    start, ltop, lbot, ra, rb = kernel(
        near_kernel,
        [local, own, rest, twin, cross],
        [(height, width)] + [((height, 4 * span), BF16)] * 2 + [(cross.shape, BF16)] * 2,
        [((span, width), BF16)] * 2,
        flops=1 << 31,
    )
    left, right, start = tie(left, right, start)
    far_a = moved(jnp.concatenate([firsts[0], left[:RW]], axis=0), "y", 1)
    far_b = moved(right[RW:], "y", 3)
    early = kernel(
        early_kernel,
        [start, ltop, lbot, both, left, right] + [moved(v, "c", 1) for v in (both, left, right)],
        (height, width),
        [((2 * span, width), BF16)] * 2,
        flops=1 << 31,
    )
    far_a, far_b, early = tie(far_a, far_b, early)
    *parts, kept, given = kernel(
        functools.partial(main_kernel, ALL_BLOCKS),
        [early, base, ltop, lbot, ra, rb, distant]
        + [far_a, far_b, moved(far_a, "c", 1), moved(far_b, "c", 1)],
        [(2, RW, width)] * 4 + [(tall, HALF)] * 2,
        [((span, width), BF16)] * 2
        + [((5 * RW, width), BF16)] * 2
        + [((height, width), F32)]
        + [((5 * RW, width), BF16)] * 2,
        flops=1 << 32,
    )

    got = moved(given, "c", 1)
    cut = split_sum([kept, got], at, "y")
    cols = scattered(parts, "x")
    across = scattered(cut, "y")
    keep, give = kernel(pick_kernel, cols, [(RW, width)] * 2)
    summed = moved(give, "zh", 1)
    cut = split_sum(across, at, "x")
    total = total_of(scattered(cut, "x"))
    total = total + sent(total, "zl", lambda a: a ^ 1)
    total = total + sent(total, "zl", lambda a: a ^ 2)
    total = total + moved(total, "zh", 1)
    lines = gathered(total, "x")
    total = jnp.concatenate(lines, axis=0)
    lanes = gathered(total, "y")
    twins = [moved(v, "c", 1) for v in lanes]
    return kernel(
        functools.partial(final_kernel, ALL_BLOCKS),
        lanes + twins + [keep, summed],
        [(NSUP, RW, W), (len(PAIRS), W, W), (NSUP, W, W)],
        [((tall, W), F32)],
    )


def solution(mesh):
    in_specs = (P(None, "col", None, "row"), P(None, BOTH, None), P(), P(), P(), P())
    out_specs = (P(None, BOTH, None), P(), P())

    return jax.shard_map(shards, mesh=mesh, in_specs=in_specs, out_specs=out_specs, check_vma=False)
```

```python
import functools

import jax
import jax.numpy as jnp
from jax import lax
from jax.experimental import pallas as pl
from jax.experimental.pallas import tpu as pltpu
from jax.sharding import PartitionSpec as P


W = 256
NSUP = 4
RW = 48
HALF = W // 2
SIZES = {"zh": 2, "x": 4, "y": 4, "zl": 4, "c": 2}
BOTH = ("row", "col")
F32, BF16 = jnp.float32, jnp.bfloat16
PAIRS = [(m, j) for j in range(NSUP) for m in range(j)]
ALL_BLOCKS = PAIRS + [(j, j) for j in range(NSUP)]
DIAG = len(PAIRS) * W
TALL = DIAG + 3 * W
VMEM = pl.BlockSpec(memory_space=pltpu.VMEM)
SMEM = pl.BlockSpec(memory_space=pltpu.SMEM)


def place():
    row, col = lax.axis_index("row"), lax.axis_index("col")
    return {"zh": row >> 2, "x": row & 3, "y": col >> 3, "zl": (col >> 1) & 3, "c": col & 1}


def moved(value, axis, step):
    return sent(value, axis, lambda a: (a + step) % SIZES[axis])


def sent(value, axis, rule):
    names = list(SIZES)
    perm = []
    for device in range(256):
        rest, at = device, {}
        for name in reversed(names):
            at[name] = rest % SIZES[name]
            rest //= SIZES[name]
        at[axis] = rule(at[axis])
        target = 0
        for name in names:
            target = target * SIZES[name] + at[name]
        perm.append((device, target))
    return lax.ppermute(value, BOTH, perm)


def tie(*values):
    return lax.optimization_barrier(values)


def halves(value):
    top = value.astype(BF16)
    return top, (value - top.astype(F32)).astype(BF16)


def mul(left, right, over=(1, 0)):
    dims = (((over[0],), (over[1],)), ((), ()))
    dot = lambda u, v: lax.dot_general(u, v, dims, preferred_element_type=F32)
    return dot(left[0], right[0]) + (dot(left[1], right[0]) + dot(left[0], right[1]))


def couplings(couple, parent):
    linked = {}
    blocks = {}
    for j in range(NSUP):
        for m in range(j):
            now = parent[j] == m
            for p in range(m + 1, j):
                now = now | ((parent[j] == p) & linked[p, m])
            linked[j, m] = now
            blocks[j, m] = couple[j * (j - 1) // 2 + m] * jnp.where(now, 1.0, 0.0).astype(F32)
    return blocks


def pre_kernel(parent, pattern, factor, couple, out):
    first = (lax.axis_index("row") * 32 + lax.axis_index("col")) * RW
    block = first >> 8
    after = jnp.minimum(block + 1, pattern.shape[1] - 1)
    edge = (block + 1) * W - first
    low = lax.broadcasted_iota(jnp.int32, (RW, W), 0) < edge
    blocks = couplings(couple, parent)
    values = []
    for j in range(NSUP):
        here, there = pattern[j, block].astype(F32), pattern[j, after].astype(F32)
        values.append(factor[j] * jnp.where(low, here, there))
    for m in range(NSUP):
        out[:, m * W : (m + 1) * W] = values[m]
        left = halves(values[m])
        for j in range(m + 1, NSUP):
            values[j] = values[j] - mul(left, halves(blocks[j, m]))


def base_table(order):
    at = lambda q, j: order.index((q, j))
    return [(at(m, j), at(q, m), at(q, j)) for j in range(NSUP) for m in range(j + 1) for q in range(m)]


def base_kernel(order, parent, table, couple, diag_inv, out, *held):
    chigh, clow, ihigh, ilow, shigh, slow = held
    at = lambda q, j: order.index((q, j))

    def keep(high, low, i, value):
        high[i], low[i] = halves(value)

    def kept(high, low, i):
        return high[i], low[i]

    for (j, m), value in couplings(couple, parent).items():
        keep(chigh, clow, at(m, j), value)
        keep(ihigh, ilow, at(m, j), -value)
    for gap in range(2, NSUP):
        for m in range(NSUP - gap):
            j = m + gap
            value = -(chigh[at(m, j)].astype(F32) + clow[at(m, j)].astype(F32))
            for q in range(m + 1, j):
                value = value - mul(kept(ihigh, ilow, at(m, q)), kept(chigh, clow, at(q, j)))
            keep(ihigh, ilow, at(m, j), value)
    for q in range(NSUP):
        out[at(q, q) * W : (at(q, q) + 1) * W, :] = diag_inv[q]
        keep(shigh, slow, at(q, q), diag_inv[q])
        for j in range(q + 1, NSUP):
            i = at(q, j)
            value = mul(kept(shigh, slow, at(q, q)), kept(ihigh, ilow, i))
            out[i * W : (i + 1) * W, :] = value
            keep(shigh, slow, i, value)

    def gain(t, carry):
        where = pl.ds(pl.multiple_of(table[t, 0] * W, W), W)
        left, right = kept(ihigh, ilow, table[t, 1]), kept(shigh, slow, table[t, 2])
        out[where, :] = out[where, :] + mul(left, right, (0, 0))
        return carry

    lax.fori_loop(0, len(base_table(order)), gain, 0)


def put(piece, top, bot, row_of, weight=None):
    def step(r, carry):
        src = pl.multiple_of(r * RW, 16)
        dst = pl.multiple_of(row_of(r), 16)
        value = piece[pl.ds(src, RW), :]
        hi, lo = halves(value if weight is None else value * weight(r))
        top[pl.ds(dst, RW), :] = hi
        bot[pl.ds(dst, RW), :] = lo
        return carry

    lax.fori_loop(0, piece.shape[0] // RW, step, 0)


def near_kernel(local, own, rest, twin, cross, out, ltop, lbot, rtop, rbot, top, bot):
    at = place()
    span = local.shape[1] // 4
    for i, k in enumerate((0, 1, 3, 2)):
        src = pl.multiple_of(((at["y"] - k) & 3) * span, 128)

        def step(t, carry, src=src, i=i):
            rows = pl.ds(pl.multiple_of(t * RW, 16), RW)
            hi, lo = halves(local[rows, pl.ds(src, span)])
            ltop[rows, i * span : (i + 1) * span] = hi
            lbot[rows, i * span : (i + 1) * span] = lo
            return carry

        lax.fori_loop(0, local.shape[0] // RW, step, 0)
    put(cross, rtop, rbot, lambda r: r * RW, lambda r: jnp.where(r == 1, 1.0, 0.5).astype(F32))
    for piece, par, skip in ((own, 0, 0), (rest, 0, 1), (twin, 1, 0)):
        core = at["c"] ^ par
        put(piece, top, bot, lambda r: (((at["zl"] - r - skip) & 3) * 2 + core) * RW)
    out[...] = mul((ltop[:, :span], lbot[:, :span]), (top[...], bot[...]))


def early_kernel(start, ltop, lbot, *refs):
    pieces, (out, top, bot) = refs[:6], refs[6:]
    at = place()
    span = ltop.shape[1] // 4
    for i, piece in enumerate(pieces):
        core = at["c"] ^ (i // 3)
        if i % 3 == 0:
            put(piece, top, bot, lambda r: (r * 8 + at["zl"] * 2 + core) * RW)
        else:
            side = i % 3 - 1
            put(piece, top, bot, lambda r: (side * 8 + ((at["zl"] - r - 1) & 3) * 2 + core) * RW)
    cols = slice(span, 3 * span)
    out[...] = start[...] + mul((ltop[:, cols], lbot[:, cols]), (top[...], bot[...]))


def main_kernel(*refs):
    early, ltop, lbot, ra, rb, distant = refs[:6]
    pieces, outs = refs[6:10], refs[10:14]
    kept, given = refs[14], refs[15]
    top, bot, rtop, rbot, result, ptop, pbot = refs[16:]
    at = place()
    span = ltop.shape[1] // 4
    quad = ra.shape[0]
    for i, piece in enumerate(pieces):
        core = at["c"] ^ (i // 2)
        start = 2 * (i % 2)
        put(piece, top, bot, lambda r: (((at["zl"] - r - start) & 3) * 2 + core) * RW)
    rtop[:quad, :] = ra[...]
    rbot[:quad, :] = rb[...]
    put(distant, rtop, rbot, lambda r: quad + r * RW)
    cols = slice(3 * span, 4 * span)
    value = early[...] + mul((ltop[:, cols], lbot[:, cols]), (top[...], bot[...]))
    result[...] = value
    taken = [at["zh"] * 4 + ((at["x"] + k) & 3) for k in range(3)]
    taken += [(1 - at["zh"]) * 4 + ((at["x"] + k + at["zh"]) & 3) for k in range(2)]
    for i, block in enumerate(taken):
        hi, lo = halves(result[pl.ds(pl.multiple_of(block * RW, 16), RW), :])
        ptop[i * RW : (i + 1) * RW, :] = hi
        pbot[i * RW : (i + 1) * RW, :] = lo
    for k, out in enumerate(outs):
        xa = (at["x"] + k) & 3
        for r in range(2):
            out[r] = result[pl.ds(pl.multiple_of((r * 4 + xa) * RW, 16), RW), :]
    even = at["c"] == 0

    def share(row, zero, one):
        rows = slice(row, row + zero.shape[0])
        kept[rows, :] = jnp.where(even, zero, one)
        given[rows, :] = jnp.where(even, one, zero)

    def factors(s):
        cols = slice(s * W, (s + 1) * W)
        return (rtop[:, cols], rbot[:, cols]), (ptop[:, cols], pbot[:, cols])

    for i, (m, j) in enumerate(PAIRS):
        (row_m, part_m), (row_j, part_j) = factors(m), factors(j)
        block = mul(row_m, part_j, (0, 0)) + mul(part_m, row_j, (0, 0))
        share(i * W, block[:, :HALF], block[:, HALF:])
    for t in range(2):
        here, there = (mul(*factors(s), (0, 0)) for s in (t, t + 2))
        here, there = here + here.T, there + there.T
        share(DIAG + t * W, here[:, :HALF], there[:, HALF:])
        share(DIAG + 2 * W + t * HALF, there[:HALF, :HALF], here[HALF:, HALF:])


def pick_kernel(*refs):
    pieces, keep, give = refs[:4], refs[4], refs[5]
    zh = place()["zh"]
    for out, side in ((keep, zh), (give, 1 - zh)):
        total = pieces[0][side]
        for piece in pieces[1:]:
            total = total + piece[side]
        out[...] = total


def final_kernel(*refs):
    pieces, (keep, got, base) = refs[:8], refs[8:11]
    columns, pair_out, diag_out, whole = refs[11:]
    at = place()
    rows = pieces[0].shape[0]
    small = rows // 4
    for i, piece in enumerate(pieces):
        par, k = divmod(i, 4)
        for r in range(4):
            dst = pl.multiple_of(((at["y"] - k) & 3) * rows + ((at["x"] - r) & 3) * small, 8)
            whole[at["c"] ^ par, pl.ds(dst, small), :] = piece[r * small : (r + 1) * small, :]
    left, right = slice(0, HALF), slice(HALF, W)
    for p in range(len(PAIRS)):
        span = slice(p * W, (p + 1) * W)
        pair_out[p, :, left] = whole[0, span, :] + base[span, left]
        pair_out[p, :, right] = whole[1, span, :] + base[span, right]
    for t in range(2):
        full = slice(DIAG + t * W, DIAG + (t + 1) * W)
        quarter = slice(DIAG + 2 * W + t * HALF, DIAG + 2 * W + (t + 1) * HALF)
        upper, lower = (base.at[DIAG + s * W : DIAG + (s + 1) * W, :] for s in (t, t + 2))
        side = whole[0, full, :]
        diag_out[t, :, left] = side + upper[:, left]
        diag_out[t, :HALF, right] = side[HALF:, :].T + upper[:HALF, right]
        diag_out[t, HALF:, right] = whole[1, quarter, :] + upper[HALF:, right]
        side = whole[1, full, :]
        diag_out[t + 2, :, right] = side + lower[:, right]
        diag_out[t + 2, HALF:, left] = side[:HALF, :].T + lower[HALF:, left]
        diag_out[t + 2, :HALF, left] = whole[0, quarter, :] + lower[:HALF, left]
    for j in range(NSUP):
        cols = slice(j * W, (j + 1) * W)
        columns[j] = -(keep[:, cols] + got[:, cols])


def kernel(body, args, out_shapes, scratch=(), smem=0, flops=0):
    single = not isinstance(out_shapes, list)
    return pl.pallas_call(
        body,
        out_shape=jax.ShapeDtypeStruct(out_shapes, F32)
        if single
        else [jax.ShapeDtypeStruct(s, F32) if isinstance(s[-1], int) else jax.ShapeDtypeStruct(*s) for s in out_shapes],
        in_specs=[SMEM] * smem + [VMEM] * (len(args) - smem),
        out_specs=VMEM if single else [VMEM] * len(out_shapes),
        scratch_shapes=[pltpu.VMEM(s, t) for s, t in scratch],
        compiler_params=pltpu.CompilerParams(vmem_limit_bytes=56 << 20),
        cost_estimate=pl.CostEstimate(
            flops=flops, transcendentals=0, bytes_accessed=sum(4 * a.size for a in args)
        ),
    )(*args)


def split_sum(values, at, axis):
    n = SIZES[axis]
    rows = values[0].shape[0] // n
    part = lambda v, k: lax.dynamic_slice_in_dim(v, ((at[axis] + k) & (n - 1)) * rows, rows, 0)
    return [total_of([part(v, k) for v in values]) for k in range(n)]


def scattered(pieces, axis):
    return [pieces[0]] + [moved(pieces[k], axis, k) for k in range(1, len(pieces))]


def gathered(value, axis):
    return [value] + [moved(value, axis, k) for k in range(1, SIZES[axis])]


def total_of(values):
    total = values[0]
    for value in values[1:]:
        total = total + value
    return total


def shards(inv_anc, factor_cols, couple, diag_inv, pattern, parent):
    at = place()
    local = inv_anc.reshape(-1, inv_anc.shape[3])
    height = local.shape[0]

    own = kernel(
        pre_kernel, [parent, pattern, factor_cols, couple], (RW, NSUP * W), smem=2, flops=1 << 20
    )
    width = NSUP * W
    tall = len(ALL_BLOCKS) * W
    span = local.shape[1] // 4

    near = gathered(own, "zl")
    firsts = [moved(own, "y", 1), moved(own, "y", 3)]
    cross = [own, moved(own, "x", 3), moved(own, "x", 2)]
    _, couple_later = tie(own, couple)
    base = kernel(
        functools.partial(base_kernel, ALL_BLOCKS),
        [parent, jnp.array(base_table(ALL_BLOCKS), jnp.int32), couple_later, diag_inv],
        (tall, W),
        [((len(ALL_BLOCKS), W, W), BF16)] * 6,
        smem=2,
        flops=1 << 31,
    )
    rest = jnp.concatenate(near[1:], axis=0)
    both = jnp.concatenate(firsts, axis=0)
    cross, both = tie(jnp.concatenate(cross, axis=0), both)

    left, right = moved(rest, "y", 1), moved(rest, "y", 3)
    distant = moved(lax.dynamic_slice_in_dim(cross, (1 - at["zh"]) * RW, 2 * RW, 0), "zh", 1)
    twin = moved(jnp.concatenate([own, rest], axis=0), "c", 1)
    start, ltop, lbot, ra, rb = kernel(
        near_kernel,
        [local, own, rest, twin, cross],
        [(height, width)] + [((height, 4 * span), BF16)] * 2 + [(cross.shape, BF16)] * 2,
        [((span, width), BF16)] * 2,
        flops=1 << 31,
    )
    left, right, start = tie(left, right, start)
    far_a = moved(jnp.concatenate([firsts[0], left[:RW]], axis=0), "y", 1)
    far_b = moved(right[RW:], "y", 3)
    both2 = moved(both, "c", 1)
    left2, right2 = moved(left, "c", 1), moved(right, "c", 1)
    early = kernel(
        early_kernel,
        [start, ltop, lbot, both, left, right, both2, left2, right2],
        (height, width),
        [((2 * span, width), BF16)] * 2,
        flops=1 << 31,
    )
    far_a, far_b, early = tie(far_a, far_b, early)
    *parts, kept, given = kernel(
        main_kernel,
        [early, ltop, lbot, ra, rb, distant]
        + [far_a, far_b, moved(far_a, "c", 1), moved(far_b, "c", 1)],
        [(2, RW, width)] * 4 + [(TALL, HALF)] * 2,
        [((span, width), BF16)] * 2
        + [((5 * RW, width), BF16)] * 2
        + [((height, width), F32)]
        + [((5 * RW, width), BF16)] * 2,
        flops=1 << 32,
    )

    got = moved(given, "c", 1)
    cut = split_sum([kept, got], at, "y")
    cols = scattered(parts, "x")
    across = scattered(cut, "y")
    keep, give = kernel(pick_kernel, cols, [(RW, width)] * 2)
    summed = moved(give, "zh", 1)
    cut = split_sum(across, at, "x")
    total = total_of(scattered(cut, "x"))
    total = total + sent(total, "zl", lambda a: a ^ 1)
    total = total + sent(total, "zl", lambda a: a ^ 2)
    total = total + moved(total, "zh", 1)
    lines = gathered(total, "x")
    total = jnp.concatenate(lines, axis=0)
    lanes = gathered(total, "y")
    twins = [moved(v, "c", 1) for v in lanes]
    return kernel(
        final_kernel,
        lanes + twins + [keep, summed, base],
        [(NSUP, RW, W), (len(PAIRS), W, W), (NSUP, W, W)],
        [((2, TALL, HALF), F32)],
    )


def solution(mesh):
    in_specs = (P(None, "col", None, "row"), P(None, BOTH, None), P(), P(), P(), P())
    out_specs = (P(None, BOTH, None), P(), P())

    return jax.shard_map(shards, mesh=mesh, in_specs=in_specs, out_specs=out_specs, check_vma=False)
```

```python
import functools

import jax
import jax.numpy as jnp
from jax import lax
from jax.experimental import pallas as pl
from jax.experimental.pallas import tpu as pltpu
from jax.sharding import PartitionSpec as P


W = 256
NSUP = 4
RW = 48
HALF = W // 2
SIZES = {"zh": 2, "x": 4, "y": 4, "zl": 4, "c": 2}
BOTH = ("row", "col")
F32, BF16 = jnp.float32, jnp.bfloat16
PAIRS = [(m, j) for j in range(NSUP) for m in range(j)]
ALL_BLOCKS = PAIRS + [(j, j) for j in range(NSUP)]
DIAG = len(PAIRS) * W
TALL = DIAG + 3 * W
VMEM = pl.BlockSpec(memory_space=pltpu.VMEM)
SMEM = pl.BlockSpec(memory_space=pltpu.SMEM)


def place():
    row, col = lax.axis_index("row"), lax.axis_index("col")
    return {"zh": row >> 2, "x": row & 3, "y": col >> 3, "zl": (col >> 1) & 3, "c": col & 1}


def moved(value, axis, step):
    return sent(value, axis, lambda a: (a + step) % SIZES[axis])


def sent(value, axis, rule):
    names = list(SIZES)
    perm = []
    for device in range(256):
        rest, at = device, {}
        for name in reversed(names):
            at[name] = rest % SIZES[name]
            rest //= SIZES[name]
        at[axis] = rule(at[axis])
        target = 0
        for name in names:
            target = target * SIZES[name] + at[name]
        perm.append((device, target))
    return lax.ppermute(value, BOTH, perm)


def tie(*values):
    return lax.optimization_barrier(values)


def halves(value):
    top = value.astype(BF16)
    return top, (value - top.astype(F32)).astype(BF16)


def mul(left, right, over=(1, 0)):
    dims = (((over[0],), (over[1],)), ((), ()))
    dot = lambda u, v: lax.dot_general(u, v, dims, preferred_element_type=F32)
    return dot(left[0], right[0]) + (dot(left[1], right[0]) + dot(left[0], right[1]))


def couplings(couple, parent):
    linked = {}
    blocks = {}
    for j in range(NSUP):
        for m in range(j):
            now = parent[j] == m
            for p in range(m + 1, j):
                now = now | ((parent[j] == p) & linked[p, m])
            linked[j, m] = now
            blocks[j, m] = couple[j * (j - 1) // 2 + m] * jnp.where(now, 1.0, 0.0).astype(F32)
    return blocks


def pre_kernel(parent, pattern, factor, couple, out):
    first = (lax.axis_index("row") * 32 + lax.axis_index("col")) * RW
    block = first >> 8
    after = jnp.minimum(block + 1, pattern.shape[1] - 1)
    edge = (block + 1) * W - first
    low = lax.broadcasted_iota(jnp.int32, (RW, W), 0) < edge
    blocks = couplings(couple, parent)
    values = []
    for j in range(NSUP):
        here, there = pattern[j, block].astype(F32), pattern[j, after].astype(F32)
        values.append(factor[j] * jnp.where(low, here, there))
    for m in range(NSUP):
        out[:, m * W : (m + 1) * W] = values[m]
        left = halves(values[m])
        for j in range(m + 1, NSUP):
            values[j] = values[j] - mul(left, halves(blocks[j, m]))


def base_table(order):
    at = lambda q, j: order.index((q, j))
    return [(at(m, j), at(q, m), at(q, j)) for j in range(NSUP) for m in range(j + 1) for q in range(m)]


def base_kernel(order, parent, table, couple, diag_inv, out, *held):
    chigh, clow, ihigh, ilow, shigh, slow = held
    at = lambda q, j: order.index((q, j))

    def keep(high, low, i, value):
        high[i], low[i] = halves(value)

    def kept(high, low, i):
        return high[i], low[i]

    for (j, m), value in couplings(couple, parent).items():
        keep(chigh, clow, at(m, j), value)
        keep(ihigh, ilow, at(m, j), -value)
    for gap in range(2, NSUP):
        for m in range(NSUP - gap):
            j = m + gap
            value = -(chigh[at(m, j)].astype(F32) + clow[at(m, j)].astype(F32))
            for q in range(m + 1, j):
                value = value - mul(kept(ihigh, ilow, at(m, q)), kept(chigh, clow, at(q, j)))
            keep(ihigh, ilow, at(m, j), value)
    for q in range(NSUP):
        out[at(q, q) * W : (at(q, q) + 1) * W, :] = diag_inv[q]
        keep(shigh, slow, at(q, q), diag_inv[q])
        for j in range(q + 1, NSUP):
            i = at(q, j)
            value = mul(kept(shigh, slow, at(q, q)), kept(ihigh, ilow, i))
            out[i * W : (i + 1) * W, :] = value
            keep(shigh, slow, i, value)

    def gain(t, carry):
        where = pl.ds(pl.multiple_of(table[t, 0] * W, W), W)
        left, right = kept(ihigh, ilow, table[t, 1]), kept(shigh, slow, table[t, 2])
        out[where, :] = out[where, :] + mul(left, right, (0, 0))
        return carry

    lax.fori_loop(0, len(base_table(order)), gain, 0)


def put(piece, top, bot, row_of, weight=None):
    def step(r, carry):
        src = pl.multiple_of(r * RW, 16)
        dst = pl.multiple_of(row_of(r), 16)
        value = piece[pl.ds(src, RW), :]
        hi, lo = halves(value if weight is None else value * weight(r))
        top[pl.ds(dst, RW), :] = hi
        bot[pl.ds(dst, RW), :] = lo
        return carry

    lax.fori_loop(0, piece.shape[0] // RW, step, 0)


def near_kernel(local, own, rest, twin, cross, out, ltop, lbot, rtop, rbot, top, bot):
    at = place()
    span = local.shape[1] // 4
    for i, k in enumerate((0, 1, 3, 2)):
        src = pl.multiple_of(((at["y"] - k) & 3) * span, 128)

        def step(t, carry, src=src, i=i):
            rows = pl.ds(pl.multiple_of(t * RW, 16), RW)
            hi, lo = halves(local[rows, pl.ds(src, span)])
            ltop[rows, i * span : (i + 1) * span] = hi
            lbot[rows, i * span : (i + 1) * span] = lo
            return carry

        lax.fori_loop(0, local.shape[0] // RW, step, 0)
    put(cross, rtop, rbot, lambda r: r * RW, lambda r: jnp.where(r == 1, 1.0, 0.5).astype(F32))
    for piece, par, skip in ((own, 0, 0), (rest, 0, 1), (twin, 1, 0)):
        core = at["c"] ^ par
        put(piece, top, bot, lambda r: (((at["zl"] - r - skip) & 3) * 2 + core) * RW)
    out[...] = mul((ltop[:, :span], lbot[:, :span]), (top[...], bot[...]))


def early_kernel(start, ltop, lbot, *refs):
    pieces, (out, top, bot) = refs[:6], refs[6:]
    at = place()
    span = ltop.shape[1] // 4
    for i, piece in enumerate(pieces):
        core = at["c"] ^ (i // 3)
        if i % 3 == 0:
            put(piece, top, bot, lambda r: (r * 8 + at["zl"] * 2 + core) * RW)
        else:
            side = i % 3 - 1
            put(piece, top, bot, lambda r: (side * 8 + ((at["zl"] - r - 1) & 3) * 2 + core) * RW)
    cols = slice(span, 3 * span)
    out[...] = start[...] + mul((ltop[:, cols], lbot[:, cols]), (top[...], bot[...]))


def main_kernel(*refs):
    early, ltop, lbot, ra, rb, distant = refs[:6]
    pieces, outs = refs[6:10], refs[10:14]
    kept, given = refs[14], refs[15]
    top, bot, rtop, rbot, result, ptop, pbot = refs[16:]
    at = place()
    span = ltop.shape[1] // 4
    quad = ra.shape[0]
    for i, piece in enumerate(pieces):
        core = at["c"] ^ (i // 2)
        start = 2 * (i % 2)
        put(piece, top, bot, lambda r: (((at["zl"] - r - start) & 3) * 2 + core) * RW)
    rtop[:quad, :] = ra[...]
    rbot[:quad, :] = rb[...]
    put(distant, rtop, rbot, lambda r: quad + r * RW)
    cols = slice(3 * span, 4 * span)
    value = early[...] + mul((ltop[:, cols], lbot[:, cols]), (top[...], bot[...]))
    result[...] = value
    taken = [at["zh"] * 4 + ((at["x"] + k) & 3) for k in range(3)]
    taken += [(1 - at["zh"]) * 4 + ((at["x"] + k + at["zh"]) & 3) for k in range(2)]
    for i, block in enumerate(taken):
        hi, lo = halves(result[pl.ds(pl.multiple_of(block * RW, 16), RW), :])
        ptop[i * RW : (i + 1) * RW, :] = hi
        pbot[i * RW : (i + 1) * RW, :] = lo
    for k, out in enumerate(outs):
        xa = (at["x"] + k) & 3
        for r in range(2):
            out[r] = result[pl.ds(pl.multiple_of((r * 4 + xa) * RW, 16), RW), :]
    even = at["c"] == 0

    def share(row, zero, one):
        rows = slice(row, row + zero.shape[0])
        kept[rows, :] = jnp.where(even, zero, one)
        given[rows, :] = jnp.where(even, one, zero)

    def factors(s):
        cols = slice(s * W, (s + 1) * W)
        return (rtop[:, cols], rbot[:, cols]), (ptop[:, cols], pbot[:, cols])

    for i, (m, j) in enumerate(PAIRS):
        (row_m, part_m), (row_j, part_j) = factors(m), factors(j)
        block = mul(row_m, part_j, (0, 0)) + mul(part_m, row_j, (0, 0))
        share(i * W, block[:, :HALF], block[:, HALF:])
    for t in range(2):
        here, there = (mul(*factors(s), (0, 0)) for s in (t, t + 2))
        here, there = here + here.T, there + there.T
        share(DIAG + t * W, here[:, :HALF], there[:, HALF:])
        share(DIAG + 2 * W + t * HALF, there[:HALF, :HALF], here[HALF:, HALF:])


def pick_kernel(*refs):
    pieces, keep, give = refs[:4], refs[4], refs[5]
    zh = place()["zh"]
    for out, side in ((keep, zh), (give, 1 - zh)):
        total = pieces[0][side]
        for piece in pieces[1:]:
            total = total + piece[side]
        out[...] = total


def final_kernel(*refs):
    pieces, (keep, got, base) = refs[:8], refs[8:11]
    columns_out, pair_out, diag_out, whole, columns, pairs, diags, done = refs[11:]
    at = place()
    copies = []

    def write(source, target):
        copy = pltpu.make_async_copy(source, target, done.at[len(copies)])
        copy.start()
        copies.append(copy)

    for j in range(NSUP):
        cols = slice(j * W, (j + 1) * W)
        columns[j] = -(keep[:, cols] + got[:, cols])
    write(columns, columns_out)
    rows = pieces[0].shape[0]
    small = rows // 4
    for i, piece in enumerate(pieces):
        par, k = divmod(i, 4)
        for r in range(4):
            dst = pl.multiple_of(((at["y"] - k) & 3) * rows + ((at["x"] - r) & 3) * small, 8)
            whole[at["c"] ^ par, pl.ds(dst, small), :] = piece[r * small : (r + 1) * small, :]
    left, right = slice(0, HALF), slice(HALF, W)
    for t in range(2):
        full = slice(DIAG + t * W, DIAG + (t + 1) * W)
        quarter = slice(DIAG + 2 * W + t * HALF, DIAG + 2 * W + (t + 1) * HALF)
        upper, lower = (base.at[DIAG + s * W : DIAG + (s + 1) * W, :] for s in (t, t + 2))
        side = whole[0, full, :]
        diags[t, :, left] = side + upper[:, left]
        diags[t, :HALF, right] = side[HALF:, :].T + upper[:HALF, right]
        diags[t, HALF:, right] = whole[1, quarter, :] + upper[HALF:, right]
        write(diags.at[t], diag_out.at[t])
        side = whole[1, full, :]
        diags[t + 2, :, right] = side + lower[:, right]
        diags[t + 2, HALF:, left] = side[:HALF, :].T + lower[HALF:, left]
        diags[t + 2, :HALF, left] = whole[0, quarter, :] + lower[:HALF, left]
        write(diags.at[t + 2], diag_out.at[t + 2])
    for p in range(len(PAIRS)):
        span = slice(p * W, (p + 1) * W)
        pairs[p, :, left] = whole[0, span, :] + base[span, left]
        pairs[p, :, right] = whole[1, span, :] + base[span, right]
        write(pairs.at[p], pair_out.at[p])
    for copy in copies:
        copy.wait()


def kernel(body, args, out_shapes, scratch=(), smem=0, flops=0):
    single = not isinstance(out_shapes, list)
    return pl.pallas_call(
        body,
        out_shape=jax.ShapeDtypeStruct(out_shapes, F32)
        if single
        else [jax.ShapeDtypeStruct(s, F32) if isinstance(s[-1], int) else jax.ShapeDtypeStruct(*s) for s in out_shapes],
        in_specs=[SMEM] * smem + [VMEM] * (len(args) - smem),
        out_specs=VMEM if single else [VMEM] * len(out_shapes),
        scratch_shapes=[pltpu.VMEM(s, t) for s, t in scratch],
        compiler_params=pltpu.CompilerParams(vmem_limit_bytes=56 << 20),
        cost_estimate=pl.CostEstimate(
            flops=flops, transcendentals=0, bytes_accessed=sum(4 * a.size for a in args)
        ),
    )(*args)


def split_sum(values, at, axis):
    n = SIZES[axis]
    rows = values[0].shape[0] // n
    part = lambda v, k: lax.dynamic_slice_in_dim(v, ((at[axis] + k) & (n - 1)) * rows, rows, 0)
    return [total_of([part(v, k) for v in values]) for k in range(n)]


def scattered(pieces, axis):
    return [pieces[0]] + [moved(pieces[k], axis, k) for k in range(1, len(pieces))]


def gathered(value, axis):
    return [value] + [moved(value, axis, k) for k in range(1, SIZES[axis])]


def total_of(values):
    total = values[0]
    for value in values[1:]:
        total = total + value
    return total


def shards(inv_anc, factor_cols, couple, diag_inv, pattern, parent):
    at = place()
    local = inv_anc.reshape(-1, inv_anc.shape[3])
    height = local.shape[0]

    own = kernel(
        pre_kernel, [parent, pattern, factor_cols, couple], (RW, NSUP * W), smem=2, flops=1 << 20
    )
    width = NSUP * W
    tall = len(ALL_BLOCKS) * W
    span = local.shape[1] // 4

    near = gathered(own, "zl")
    firsts = [moved(own, "y", 1), moved(own, "y", 3)]
    cross = [own, moved(own, "x", 3), moved(own, "x", 2)]
    _, couple_later = tie(own, couple)
    base = kernel(
        functools.partial(base_kernel, ALL_BLOCKS),
        [parent, jnp.array(base_table(ALL_BLOCKS), jnp.int32), couple_later, diag_inv],
        (tall, W),
        [((len(ALL_BLOCKS), W, W), BF16)] * 6,
        smem=2,
        flops=1 << 31,
    )
    rest = jnp.concatenate(near[1:], axis=0)
    both = jnp.concatenate(firsts, axis=0)
    cross, both = tie(jnp.concatenate(cross, axis=0), both)

    both2 = moved(both, "c", 1)

    left, right = moved(rest, "y", 1), moved(rest, "y", 3)
    distant = moved(lax.dynamic_slice_in_dim(cross, (1 - at["zh"]) * RW, 2 * RW, 0), "zh", 1)
    twin = moved(jnp.concatenate([own, rest], axis=0), "c", 1)
    start, ltop, lbot, ra, rb = kernel(
        near_kernel,
        [local, own, rest, twin, cross],
        [(height, width)] + [((height, 4 * span), BF16)] * 2 + [(cross.shape, BF16)] * 2,
        [((span, width), BF16)] * 2,
        flops=1 << 31,
    )
    left, right, start = tie(left, right, start)
    far_a = moved(jnp.concatenate([firsts[0], left[:RW]], axis=0), "y", 1)
    far_b = moved(right[RW:], "y", 3)
    left2, right2 = moved(left, "c", 1), moved(right, "c", 1)
    early = kernel(
        early_kernel,
        [start, ltop, lbot, both, left, right, both2, left2, right2],
        (height, width),
        [((2 * span, width), BF16)] * 2,
        flops=1 << 31,
    )
    far_a, far_b, early = tie(far_a, far_b, early)
    *parts, kept, given = kernel(
        main_kernel,
        [early, ltop, lbot, ra, rb, distant]
        + [far_a, far_b, moved(far_a, "c", 1), moved(far_b, "c", 1)],
        [(2, RW, width)] * 4 + [(TALL, HALF)] * 2,
        [((span, width), BF16)] * 2
        + [((5 * RW, width), BF16)] * 2
        + [((height, width), F32)]
        + [((5 * RW, width), BF16)] * 2,
        flops=1 << 32,
    )

    got = moved(given, "c", 1)
    cut = split_sum([kept, got], at, "y")
    cols = scattered(parts, "x")
    across = scattered(cut, "y")
    keep, give = kernel(pick_kernel, cols, [(RW, width)] * 2)
    summed = moved(give, "zh", 1)
    cut = split_sum(across, at, "x")
    total = total_of(scattered(cut, "x"))
    total = total + sent(total, "zl", lambda a: a ^ 1)
    total = total + sent(total, "zl", lambda a: a ^ 2)
    total = total + moved(total, "zh", 1)
    lines = gathered(total, "x")
    total = jnp.concatenate(lines, axis=0)
    lanes = gathered(total, "y")
    twins = [moved(v, "c", 1) for v in lanes]
    inputs = lanes + twins + [keep, summed, base]
    outs = [(NSUP, RW, W), (len(PAIRS), W, W), (NSUP, W, W)]
    return pl.pallas_call(
        final_kernel,
        out_shape=[jax.ShapeDtypeStruct(s, F32) for s in outs],
        in_specs=[VMEM] * len(inputs),
        out_specs=[pl.BlockSpec(memory_space=pl.ANY)] * 3,
        scratch_shapes=[pltpu.VMEM(s, F32) for s in [(2, TALL, HALF)] + outs]
        + [pltpu.SemaphoreType.DMA((1 + len(ALL_BLOCKS),))],
        compiler_params=pltpu.CompilerParams(vmem_limit_bytes=56 << 20),
    )(*inputs)


def solution(mesh):
    in_specs = (P(None, "col", None, "row"), P(None, BOTH, None), P(), P(), P(), P())
    out_specs = (P(None, BOTH, None), P(), P())

    return jax.shard_map(shards, mesh=mesh, in_specs=in_specs, out_specs=out_specs, check_vma=False)
```
